32 devices in a mesh: groups: 2 (over y), ctx: 4 (over z), head: 2 (over x), rep: 2 (over core).
Axes of the slice: x: 2, y: 2, z: 4, core: 2. Of those that a mesh axis runs over, the one named last changes fastest.
Arguments:
- q_self: bfloat16 [1024, 8192], P(('groups', 'ctx'), ('head', 'rep')), parts along dimension 0, may hold values from -64 to 64
- q_cross: bfloat16 [1024, 8192], P(('groups', 'ctx'), ('head', 'rep')), parts along dimension 0, may hold values from -64 to 64
- kv_self: bfloat16 [2, 1024, 1024], P(None, ('groups', 'ctx'), 'head'), parts along dimension 1, may hold values from -4 to 4
- image_kv: bfloat16 [2, 16, 1601, 1024], P(None, ('groups', 'ctx'), None, 'head'), parts along dimension 1, may hold values from -4 to 4
- cross_gate: float32 [64], P(('head', 'rep')), may hold values from -2 to 2
- doc_lengths: int32 [8], P('groups'), parts along dimension 0, may hold values from 1 to 256, 512 in all
- pair_tiles: int32 [32, 4], P(('groups', 'ctx')), parts along dimension 0, may hold values from 0 to 7, as said below
- tile_slot: int32 [16], P('groups'), parts along dimension 0, may hold values from 0 to 7, as said below
Outputs:
- mixed: bfloat16 [1024, 8192], P(('groups', 'ctx'), ('head', 'rep')), parts along dimension 0
The draws below stay inside these ranges and needn't reach their ends.
There are 2 independent parts, one for each index of `groups`. The reference program is written for one: setup_inputs(seed, part) draws one part's arguments, and reference() takes and returns one part's arrays. A program takes and returns all parts, laid end to end along the dimension named above; an argument that names none is the same for every part. Nothing has to cross between parts.
Inputs may be any that keep to these rules, and one draw needn't show every extreme that they name: `pair_tiles`: each block lists 4 tiles; a tile may be listed more than once. Over the 4 blocks of one ctx index, the pairs name tiles stored at one ctx index (slots ctx * 2 onward) at most 4 times, and at most 1 of those blocks name some tile stored there; both bounds are met in every draw, and some ctx index is named 4 times by the blocks of every ctx index. A permutation: tile i is stored at slot tile_slot[i] of image_kv.
All inputs are finite; a program needn't handle non-finite values.
Results may differ from the reference program's by a relative error of at most 0.0034.
Values may be sent and summed in bfloat16 or wider, within the bound.
No kernel may reach another device: no remote copies, remote signals or barrier semaphores. Data moves between devices by JAX's collectives and lax.ppermute only.
A program may use at most 128 MiB of HBM per device.

```python
import math
import jax
import jax.numpy as jnp
import numpy as np
from jax import lax

HEAD_DIM = 128
Q_HEADS = 64
KV_HEADS = 8
TILE_LEN = 1601
BLOCK = 32
PAIRS = 4
DOCS = 4
TOKENS = 512
NB = 16
BLK_DEV = 4
TILES_DEV = 2
TILES = 8
CAP = 4


def routing(key):
    routed_key = jax.random.fold_in(key, 101)
    perm_key, hot_key, source_key = jax.random.split(routed_key, 3)
    ctx_count = TILES // TILES_DEV
    request_count = BLK_DEV * PAIRS
    slot_table = jax.random.permutation(perm_key, TILES).astype(jnp.int32)
    tile_at_slot = jnp.zeros((TILES,), jnp.int32).at[slot_table].set(jnp.arange(TILES, dtype=jnp.int32))
    hot_owner = jax.random.randint(hot_key, (), 0, ctx_count).astype(jnp.int32)

    def one_source(sub_key):
        ranking_key, local_key = jax.random.split(sub_key)
        ranking = jax.random.permutation(ranking_key, ctx_count).astype(jnp.int32)
        where_hot = jnp.argmax((ranking == hot_owner).astype(jnp.int32))
        leader = ranking[0]
        ranking = ranking.at[where_hot].set(leader).at[0].set(hot_owner)
        owners = ranking[jnp.arange(request_count, dtype=jnp.int32) // CAP]
        picks = jax.random.randint(local_key, (request_count,), 0, TILES_DEV).astype(jnp.int32)
        return tile_at_slot[owners * TILES_DEV + picks].reshape(BLK_DEV, PAIRS)
    listed = jax.vmap(one_source)(jax.random.split(source_key, ctx_count))
    return (listed.reshape(NB, PAIRS), slot_table)


def self_keys(key):
    main_key = jax.random.fold_in(jax.random.fold_in(key, 202), 0)
    values = jnp.clip(jax.random.normal(main_key, (2, TOKENS, KV_HEADS * HEAD_DIM), jnp.float32), -4.0, 4.0)
    return values


def image_keys(key):
    main_key = jax.random.fold_in(jax.random.fold_in(key, 404), 0)
    values = jnp.clip(jax.random.normal(main_key, (2, TILES, TILE_LEN, KV_HEADS * HEAD_DIM), jnp.float32), -4.0, 4.0)
    return values


def draw_q_self(key, part):
    queries = jnp.clip(3.0 * jax.random.normal(jax.random.fold_in(key, 303), (TOKENS, Q_HEADS * HEAD_DIM), jnp.float32), -12.0, 12.0)
    return queries.astype(jnp.bfloat16)


def draw_q_cross(key, part):
    queries = jnp.clip(3.0 * jax.random.normal(jax.random.fold_in(key, 505), (TOKENS, Q_HEADS * HEAD_DIM), jnp.float32), -12.0, 12.0)
    return queries.astype(jnp.bfloat16)


def draw_kv_self(key, part):
    return self_keys(key).astype(jnp.bfloat16)


def draw_image_kv(key, part):
    return image_keys(key).astype(jnp.bfloat16)


def draw_pair_tiles(key, part):
    return routing(key)[0]


def draw_tile_slot(key, part):
    return routing(key)[1]


def block_scale(rng, dims, cuts, least, high):
    gain, own = 1.0, jax.random.fold_in(rng, 6)
    for position, parts in cuts:
        steps = jnp.exp(jax.random.uniform(jax.random.fold_in(own, position), (parts,), jnp.float32, least / len(cuts), high / len(cuts)))
        gain = gain * jnp.repeat(steps, dims[position] // parts).reshape([-1 if axis == position else 1 for axis in range(len(dims))])
    return gain


def length_profile(count, total, limit, skew):
    weights = [(1 << 20) // math.isqrt(grade ** skew) + 1 for grade in range(2, count + 1)]
    spare, holding = total - limit - (count - 1), [1] * (count - 1)
    while spare > 0:
        movable = [i for i in range(count - 1) if holding[i] < limit]
        mass, budget = sum([weights[i] for i in movable]), spare
        for i in movable:
            extra = min(limit - holding[i], max(1, budget * weights[i] // mass), spare)
            holding[i] = holding[i] + extra
            spare = spare - extra
    return np.array([limit] + holding)


def ragged_sizes(rng, amount, total, limit, slope):
    if amount == 2:
        one = jax.random.randint(rng, (), max(1, total - limit), min(limit, total - 1) + 1)
        return jnp.stack([one, total - one])
    sizes = jnp.asarray(length_profile(amount, total, limit, slope), jnp.int32)
    couples = (amount - 1) // 2
    giver, receiver = sizes[1:1 + 2 * couples:2], sizes[2:2 + 2 * couples:2]
    slack = jnp.minimum(giver - 1, limit - receiver)
    passed = jax.random.randint(jax.random.fold_in(rng, 1), (couples,), 0, 1 << 20) % (slack + 1)
    sizes = sizes.at[1:1 + 2 * couples:2].set(giver - passed).at[2:2 + 2 * couples:2].set(receiver + passed)
    return sizes[jax.random.permutation(jax.random.fold_in(rng, 2), amount)]


def setup_inputs(seed: int = 0, part: int = 0) -> dict:
    streams_of = jax.random.split(jax.random.key(seed), 9)
    own_keys = jax.random.split(jax.random.fold_in(streams_of[8], part), 9)
    return {
        "q_self": draw_q_self(jax.random.fold_in(jax.random.fold_in(streams_of[8], part), 71), part),
        "q_cross": draw_q_cross(jax.random.fold_in(jax.random.fold_in(streams_of[8], part), 71), part),
        "kv_self": draw_kv_self(jax.random.fold_in(jax.random.fold_in(streams_of[8], part), 71), part),
        "image_kv": draw_image_kv(jax.random.fold_in(jax.random.fold_in(streams_of[8], part), 71), part),
        "cross_gate": jnp.clip(jax.random.uniform(streams_of[4], (Q_HEADS,), jnp.float32, -2.0, 2.0) * block_scale(streams_of[4], (Q_HEADS,), ((0, 4),), -0.4, 0.0), -2.0, 2.0),
        "doc_lengths": ragged_sizes(own_keys[5], DOCS, TOKENS, TOKENS // 2, 2).astype(jnp.int32),
        "pair_tiles": draw_pair_tiles(jax.random.fold_in(jax.random.fold_in(streams_of[8], part), 71), part),
        "tile_slot": draw_tile_slot(jax.random.fold_in(jax.random.fold_in(streams_of[8], part), 71), part),
    }


NEG_FILL = -1.0e30


def documents(doc_lengths, positions):
    doc_ends = jnp.cumsum(doc_lengths)
    return jnp.sum((positions[:, None] >= doc_ends[None, :]).astype(jnp.int32), axis=1)


def self_attention(q_self, kv_self, doc_lengths):
    grouping = Q_HEADS // KV_HEADS
    score_scale = HEAD_DIM ** -0.5
    block_rows = math.gcd(TOKENS, 512)
    positions = jnp.arange(TOKENS, dtype=jnp.int32)
    doc_of = documents(doc_lengths, positions)
    queries = jnp.transpose(q_self.reshape(TOKENS, KV_HEADS, grouping, HEAD_DIM), (1, 0, 2, 3))
    key_rows = jnp.transpose(kv_self[0].reshape(TOKENS, KV_HEADS, HEAD_DIM), (1, 0, 2))
    value_rows = jnp.transpose(kv_self[1].reshape(TOKENS, KV_HEADS, HEAD_DIM), (1, 0, 2))

    def one_head(operands):
        head_q, head_k, head_v = operands
        keys32 = head_k.astype(jnp.float32)
        values32 = head_v.astype(jnp.float32)

        def one_block(first_row):
            block_q = lax.dynamic_slice_in_dim(head_q, first_row, block_rows, 0).astype(jnp.float32)
            block_pos = first_row + jnp.arange(block_rows, dtype=jnp.int32)
            block_doc = lax.dynamic_slice_in_dim(doc_of, first_row, block_rows, 0)
            allowed = (positions[None, :] <= block_pos[:, None]) & (doc_of[None, :] == block_doc[:, None])
            scores = jnp.einsum("tgd,nd->gtn", block_q, keys32) * score_scale
            scores = jnp.where(allowed[None], scores, NEG_FILL)
            row_best = jnp.max(scores, axis=2, keepdims=True)
            weights = jnp.where(allowed[None], jnp.exp(scores - row_best), 0.0)
            row_total = jnp.sum(weights, axis=2)
            rounded = lax.optimization_barrier(weights.astype(jnp.bfloat16)).astype(jnp.float32)
            blended = jnp.einsum("gtn,nd->tgd", rounded, values32)
            return blended / jnp.transpose(row_total)[:, :, None]

        starts = jnp.arange(0, TOKENS, block_rows, dtype=jnp.int32)
        return lax.map(one_block, starts).reshape(TOKENS, grouping, HEAD_DIM)

    head_outs = lax.map(one_head, (queries, key_rows, value_rows))
    return jnp.transpose(head_outs, (1, 0, 2, 3)).reshape(TOKENS, Q_HEADS * HEAD_DIM)


def cross_attention(q_cross, image_kv, pair_tiles, tile_slot):
    grouping = Q_HEADS // KV_HEADS
    score_scale = HEAD_DIM ** -0.5
    block_count = TOKENS // BLOCK
    stored = jnp.take(tile_slot, pair_tiles.reshape(-1), axis=0).reshape(block_count, PAIRS)
    queries = q_cross.reshape(block_count, BLOCK, KV_HEADS, grouping, HEAD_DIM)

    def one_block(operands):
        block_q, slots_read = operands
        query32 = block_q.astype(jnp.float32)

        def one_pair(slot):
            tile_k = lax.dynamic_index_in_dim(image_kv[0], slot, 0, keepdims=False)
            tile_v = lax.dynamic_index_in_dim(image_kv[1], slot, 0, keepdims=False)
            tile_k = tile_k.reshape(TILE_LEN, KV_HEADS, HEAD_DIM).astype(jnp.float32)
            tile_v = tile_v.reshape(TILE_LEN, KV_HEADS, HEAD_DIM).astype(jnp.float32)
            scores = jnp.einsum("tkgd,lkd->kgtl", query32, tile_k) * score_scale
            row_best = jnp.max(scores, axis=3)
            weights = jnp.exp(scores - row_best[..., None])
            row_total = jnp.sum(weights, axis=3)
            rounded = lax.optimization_barrier(weights.astype(jnp.bfloat16)).astype(jnp.float32)
            blended = jnp.einsum("kgtl,lkd->tkgd", rounded, tile_v)
            blended = blended / jnp.transpose(row_total, (2, 0, 1))[..., None]
            partial_value = blended.astype(jnp.bfloat16).reshape(BLOCK, Q_HEADS * HEAD_DIM)
            return partial_value, row_best + jnp.log(row_total)

        partials, tile_lse = lax.map(one_pair, slots_read)
        top_lse = jnp.max(tile_lse, axis=0, keepdims=True)
        factors = jnp.exp(tile_lse - top_lse)
        shares = factors / jnp.sum(factors, axis=0, keepdims=True)
        shares = jnp.transpose(shares, (0, 3, 1, 2))[..., None]
        pieces = partials.astype(jnp.float32).reshape(PAIRS, BLOCK, KV_HEADS, grouping, HEAD_DIM)
        return jnp.sum(shares * pieces, axis=0).reshape(BLOCK, Q_HEADS * HEAD_DIM)

    return lax.map(one_block, (queries, stored)).reshape(TOKENS, Q_HEADS * HEAD_DIM)


def reference(q_self, q_cross, kv_self, image_kv, cross_gate, doc_lengths, pair_tiles, tile_slot):
    self_out = self_attention(q_self, kv_self, doc_lengths)
    cross_out = cross_attention(q_cross, image_kv, pair_tiles, tile_slot)
    head_gate = jnp.repeat(jnp.tanh(cross_gate), HEAD_DIM)
    return (self_out + head_gate[None, :] * cross_out).astype(jnp.bfloat16)
```

```python
import functools
import math

import jax
import jax.numpy as jnp
from jax import lax
from jax.experimental import pallas as pl
from jax.experimental.pallas import tpu as pltpu
from jax.sharding import PartitionSpec as P

HEAD_DIM = 128
Q_HEADS = 64
KV_HEADS = 8
BLOCK = 32
PAIRS = 4

NEG_FILL = -1e30
META_ROWS = 16
EXP2_SCALE = HEAD_DIM ** (-0.5) * math.log2(math.e)


def owner_slots(pairs_ref, slots_ref):
    blocks, pairs = pairs_ref.shape
    return [[slots_ref[pairs_ref[b, p]] for p in range(pairs)] for b in range(blocks)]


def block_for(stored, owner, tiles_dev):
    block = jnp.int32(0)
    counts = [jnp.int32(0)] * tiles_dev
    for b, row in enumerate(stored):
        for slot in row:
            tile = slot - owner * tiles_dev
            block = jnp.where((tile >= 0) & (tile < tiles_dev), jnp.int32(b), block)
            counts = [n + (tile == i).astype(jnp.int32) for i, n in enumerate(counts)]
    return block, counts


def pack_body(where_ref, pairs_ref, slots_ref, q_ref, *out_refs, tiles_dev):
    stored = owner_slots(pairs_ref, slots_ref)
    heads = q_ref.shape[1] // HEAD_DIM
    tile_rows = lax.broadcasted_iota(jnp.int32, (META_ROWS, HEAD_DIM), 0)
    for distance, out_ref in enumerate(out_refs):
        block, counts = block_for(stored, where_ref[0] ^ distance, tiles_dev)
        rows = pl.ds(pl.multiple_of(block * BLOCK, BLOCK), BLOCK)
        for h in range(heads):
            out_ref[h * BLOCK : (h + 1) * BLOCK, :] = q_ref[rows, h * HEAD_DIM : (h + 1) * HEAD_DIM]
        meta = jnp.zeros((META_ROWS, HEAD_DIM), jnp.float32)
        for i, n in enumerate(counts):
            meta = jnp.where(tile_rows == i, n.astype(jnp.float32), meta)
        out_ref[heads * BLOCK :, :] = meta.astype(jnp.bfloat16)


def pack_queries(where, pair_tiles, tile_slot, q_cross, ctx_count, tiles_dev):
    rows = q_cross.shape[1] // HEAD_DIM * BLOCK + META_ROWS
    smem = pl.BlockSpec(memory_space=pltpu.SMEM)
    vmem = pl.BlockSpec(memory_space=pltpu.VMEM)
    return pl.pallas_call(
        functools.partial(pack_body, tiles_dev=tiles_dev),
        out_shape=[jax.ShapeDtypeStruct((rows, HEAD_DIM), jnp.bfloat16)] * ctx_count,
        in_specs=[smem, smem, smem, vmem],
        out_specs=[vmem] * ctx_count,
        name="pack_queries",
    )(where, pair_tiles, tile_slot, q_cross)


def tile_body(where_ref, q_ref, meta_ref, k_ref, v_ref, out_ref, lse_ref, best_sc, total_sc, sum_sc):
    tile = pl.program_id(1)

    @pl.when(tile == 0)
    def _():
        best_sc[...] = jnp.full(best_sc.shape, NEG_FILL, jnp.float32)
        total_sc[...] = jnp.zeros(total_sc.shape, jnp.float32)
        sum_sc[...] = jnp.zeros(sum_sc.shape, jnp.float32)

    scores = lax.dot_general(
        q_ref[...], k_ref[0, 0], (((1,), (1,)), ((), ())), preferred_element_type=jnp.float32
    )
    row_best = jnp.max(scores, axis=1, keepdims=True)
    weights = jnp.exp2((scores - row_best) * EXP2_SCALE)
    row_total = jnp.sum(weights, axis=1, keepdims=True)
    blended = jnp.dot(weights.astype(jnp.bfloat16), v_ref[0, 0], preferred_element_type=jnp.float32)
    meta = meta_ref[...].astype(jnp.float32)
    tile_rows = lax.broadcasted_iota(jnp.int32, meta.shape, 0)
    count = jnp.sum(jnp.where(tile_rows == tile, meta, 0.0), axis=0, keepdims=True)
    row_best = jnp.where(count > 0, row_best, NEG_FILL)
    old_best = best_sc[...]
    new_best = jnp.maximum(old_best, row_best)
    fading = jnp.exp2((old_best - new_best) * EXP2_SCALE)
    share = count * jnp.exp2((row_best - new_best) * EXP2_SCALE)
    best_sc[...] = new_best
    total_sc[...] = total_sc[...] * fading + row_total * share
    sum_sc[...] = sum_sc[...] * fading + blended * share

    @pl.when(tile == pl.num_programs(1) - 1)
    def _():
        total = total_sc[...]
        live = total > 0
        total = jnp.where(live, total, 1.0)
        out_ref[...] = (sum_sc[...] / total).astype(jnp.bfloat16)
        if lse_ref is not None:
            lse = best_sc[...] * (HEAD_DIM ** (-0.5)) + jnp.log(total)
            lse_ref[...] = jnp.where(live, lse, NEG_FILL)


def attend_tiles(where, packed, image_kv, kv_used, with_lse):
    tiles_dev, tile_len = image_kv.shape[1:3]
    q_rows = packed.shape[0] - META_ROWS
    rows = q_rows // kv_used
    meta_at = q_rows // META_ROWS
    out_spec = pl.BlockSpec((rows, HEAD_DIM), lambda k, i, w: (k, 0))
    out_specs = [out_spec]
    out_shape = [jax.ShapeDtypeStruct((q_rows, HEAD_DIM), jnp.bfloat16)]
    body = tile_body
    if with_lse:
        out_specs.append(out_spec)
        out_shape.append(jax.ShapeDtypeStruct((q_rows, HEAD_DIM), jnp.float32))
    else:
        body = lambda *refs: tile_body(*refs[:6], None, *refs[6:])
    return pl.pallas_call(
        body,
        out_shape=out_shape,
        grid_spec=pltpu.PrefetchScalarGridSpec(
            num_scalar_prefetch=1,
            grid=(kv_used, tiles_dev),
            in_specs=[
                pl.BlockSpec((rows, HEAD_DIM), lambda k, i, w: (k, 0)),
                pl.BlockSpec((META_ROWS, HEAD_DIM), lambda k, i, w: (meta_at, 0)),
                pl.BlockSpec((1, 1, tile_len, HEAD_DIM), lambda k, i, w: (0, i, 0, w[1] + k)),
                pl.BlockSpec((1, 1, tile_len, HEAD_DIM), lambda k, i, w: (1, i, 0, w[1] + k)),
            ],
            out_specs=out_specs,
            scratch_shapes=[pltpu.VMEM((rows, HEAD_DIM), jnp.float32)] * 3,
        ),
        name="attend_tiles",
    )(where, packed, packed, image_kv, image_kv)


def self_body(where_ref, docs_ref, q_ref, *refs):
    kv_refs, out_ref = refs[:-1], refs[-1]
    tok_rows = q_ref.shape[0]
    keys = jnp.concatenate([ref[0] for ref in kv_refs], axis=0)
    values = jnp.concatenate([ref[1] for ref in kv_refs], axis=0)
    shape = (tok_rows, keys.shape[0])
    row_start = where_ref[0] * tok_rows
    query_pos = row_start + lax.broadcasted_iota(jnp.int32, shape, 0)
    key_pos = row_start + tok_rows - shape[1] + lax.broadcasted_iota(jnp.int32, shape, 1)
    doc_start = jnp.zeros(shape, jnp.int32)
    doc_end = jnp.int32(0)
    for j in range(docs_ref.shape[0]):
        doc_end = doc_end + docs_ref[j]
        doc_start = jnp.where(query_pos >= doc_end, doc_end, doc_start)
    allowed = (key_pos <= query_pos) & (key_pos >= doc_start)
    for g in range(q_ref.shape[1] // HEAD_DIM):
        cols = slice(g * HEAD_DIM, (g + 1) * HEAD_DIM)
        scores = lax.dot_general(
            q_ref[:, cols], keys, (((1,), (1,)), ((), ())), preferred_element_type=jnp.float32
        )
        scores = jnp.where(allowed, scores, NEG_FILL)
        row_best = jnp.max(scores, axis=1, keepdims=True)
        weights = jnp.exp2((scores - row_best) * EXP2_SCALE)
        weights = jnp.where(allowed, weights, 0.0)
        row_total = jnp.sum(weights, axis=1, keepdims=True)
        blended = jnp.dot(weights.astype(jnp.bfloat16), values, preferred_element_type=jnp.float32)
        out_ref[:, cols] = blended / row_total


def attend_self(where, doc_lengths, q_self, pieces, kv_self, kv_used, per_kv):
    tok_rows, q_width = q_self.shape
    piece_spec = pl.BlockSpec((2, tok_rows, HEAD_DIM), lambda k, w, d: (0, 0, k))
    own_spec = pl.BlockSpec((2, tok_rows, HEAD_DIM), lambda k, w, d: (0, 0, w[1] + k))
    q_spec = pl.BlockSpec((tok_rows, per_kv * HEAD_DIM), lambda k, w, d: (0, k))
    return pl.pallas_call(
        self_body_call,
        out_shape=jax.ShapeDtypeStruct((tok_rows, q_width), jnp.float32),
        grid_spec=pltpu.PrefetchScalarGridSpec(
            num_scalar_prefetch=2,
            grid=(kv_used,),
            in_specs=[q_spec] + [piece_spec] * len(pieces) + [own_spec],
            out_specs=q_spec,
        ),
        name="attend_self",
    )(where, doc_lengths, q_self, *pieces, kv_self)


def self_body_call(*refs):
    self_body(*refs)


def mix_body(where_ref, pairs_ref, slots_ref, gate_ref, self_ref, *refs, tiles_dev):
    partial_refs, out_ref = refs[:-1], refs[-1]
    stored = owner_slots(pairs_ref, slots_ref)
    for distance, partial_ref in enumerate(partial_refs):
        block, _ = block_for(stored, where_ref[0] ^ distance, tiles_dev)
        rows = pl.ds(pl.multiple_of(block * BLOCK, BLOCK), BLOCK)
        for h in range(self_ref.shape[1] // HEAD_DIM):
            cols = slice(h * HEAD_DIM, (h + 1) * HEAD_DIM)
            cross = partial_ref[h * BLOCK : (h + 1) * BLOCK, :].astype(jnp.float32)
            mixed = self_ref[rows, cols] + gate_ref[:, cols] * cross
            out_ref[rows, cols] = mixed.astype(jnp.bfloat16)


def mix(where, pair_tiles, tile_slot, gate_cols, self_out, partials, tiles_dev):
    smem = pl.BlockSpec(memory_space=pltpu.SMEM)
    vmem = pl.BlockSpec(memory_space=pltpu.VMEM)
    return pl.pallas_call(
        functools.partial(mix_body, tiles_dev=tiles_dev),
        out_shape=jax.ShapeDtypeStruct(self_out.shape, jnp.bfloat16),
        in_specs=[smem] * 3 + [vmem] * (2 + len(partials)),
        out_specs=vmem,
        name="mix",
    )(where, pair_tiles, tile_slot, gate_cols, self_out, *partials)


def mix_owners(where, pair_tiles, tile_slot, gate_cols, self_out, partials, sums, tiles_dev):
    block_count = pair_tiles.shape[0]
    tok_rows, q_width = self_out.shape
    heads = q_width // HEAD_DIM
    owners = jnp.take(tile_slot, pair_tiles.reshape(-1), axis=0).reshape(block_count, -1) // tiles_dev
    partners = where[0] ^ jnp.arange(len(partials), dtype=jnp.int32)
    live = jnp.any(owners[:, :, None] == partners[None, None, :], axis=1)[:, :, None, None]
    lse = jnp.stack(sums)[None]
    top = jnp.max(jnp.where(live, lse, NEG_FILL), axis=1, keepdims=True)
    factors = jnp.where(live, jnp.exp(lse - top), 0.0)
    pieces = jnp.stack(partials).astype(jnp.float32)[None]
    cross = jnp.sum(factors * pieces, axis=1) / jnp.sum(factors, axis=1)
    cross = jnp.transpose(cross.reshape(block_count, heads, BLOCK, HEAD_DIM), (0, 2, 1, 3))
    return (self_out + gate_cols * cross.reshape(tok_rows, q_width)).astype(jnp.bfloat16)


def local(q_self, q_cross, kv_self, image_kv, cross_gate, doc_lengths, pair_tiles, tile_slot):
    tok_rows, q_width = q_self.shape
    local_heads = q_width // HEAD_DIM
    grouping = Q_HEADS // KV_HEADS
    per_kv = min(local_heads, grouping)
    kv_used = local_heads // per_kv
    ctx_count = lax.axis_size("ctx")
    tiles_dev = image_kv.shape[1]
    request_count = pair_tiles.shape[0] * PAIRS
    capacity = max(2, -(-request_count // ctx_count))
    one_owner = ctx_count * capacity == request_count and capacity == PAIRS
    reach = min(ctx_count - 1, -(-(ctx_count * tok_rows // 2 - 1) // tok_rows))

    here = lax.axis_index("ctx").astype(jnp.int32)
    kv_first = (lax.axis_index("rep") * local_heads // grouping).astype(jnp.int32)
    where = jnp.stack([here, kv_first])

    def exchange(array, distance):
        return lax.ppermute(array, "ctx", [(i, i ^ distance) for i in range(ctx_count)])

    piece = lax.dynamic_slice_in_dim(kv_self, kv_first * HEAD_DIM, kv_used * HEAD_DIM, 2)
    pieces = []
    for step in range(reach):
        piece = lax.ppermute(piece, "ctx", [(i, i + 1) for i in range(step, ctx_count - 1)])
        pieces.insert(0, piece)

    packed = pack_queries(where, pair_tiles, tile_slot, q_cross, ctx_count, tiles_dev)
    order = list(range(ctx_count - 1, 0, -1))
    arrived = {d: exchange(packed[d], d) for d in order}
    arrived[0] = packed[0]
    partials, sums = {}, {}
    for d in [0] + order:
        results = attend_tiles(where, arrived[d], image_kv, kv_used, not one_owner)
        partials[d] = exchange(results[0], d) if d else results[0]
        if not one_owner:
            sums[d] = exchange(results[1], d) if d else results[1]
    self_out = attend_self(where, doc_lengths, q_self, pieces, kv_self, kv_used, per_kv)
    gate_cols = jnp.repeat(jnp.tanh(cross_gate), HEAD_DIM)[None, :]
    partials = [partials[d] for d in range(ctx_count)]
    if one_owner:
        return mix(where, pair_tiles, tile_slot, gate_cols, self_out, partials, tiles_dev)
    sums = [sums[d] for d in range(ctx_count)]
    return mix_owners(where, pair_tiles, tile_slot, gate_cols, self_out, partials, sums, tiles_dev)


def solution(mesh):
    in_specs = (
        P(("groups", "ctx"), ("head", "rep")),
        P(("groups", "ctx"), ("head", "rep")),
        P(None, ("groups", "ctx"), "head"),
        P(None, ("groups", "ctx"), None, "head"),
        P(("head", "rep")),
        P("groups"),
        P(("groups", "ctx"), None),
        P("groups"),
    )
    out_specs = P(("groups", "ctx"), ("head", "rep"))
    return jax.shard_map(local, mesh=mesh, in_specs=in_specs, out_specs=out_specs, check_vma=False)
```

```python
import functools
import math

import jax
import jax.numpy as jnp
from jax import lax
from jax.experimental import pallas as pl
from jax.experimental.pallas import tpu as pltpu
from jax.sharding import PartitionSpec as P

HEAD_DIM = 128
Q_HEADS = 64
KV_HEADS = 8
BLOCK = 32
PAIRS = 4

NEG_FILL = -1e30
META_ROWS = 16
KEY_CHUNK = 256
LOG2E = math.log2(math.e)
EXP2_SCALE = HEAD_DIM ** (-0.5) * LOG2E

SMEM = pl.BlockSpec(memory_space=pltpu.SMEM)
VMEM = pl.BlockSpec(memory_space=pltpu.VMEM)
ANY = pl.BlockSpec(memory_space=pl.ANY)
PARAMS = pltpu.CompilerParams(vmem_limit_bytes=24 << 20)


def in_vmem(array):
    return pltpu.with_memory_space_constraint(array, pltpu.VMEM)


def owner_slots(pairs_ref, slots_ref):
    blocks, pairs = pairs_ref.shape
    return [[slots_ref[pairs_ref[b, p]] for p in range(pairs)] for b in range(blocks)]


def block_for(stored, owner, tiles_dev):
    block = jnp.int32(0)
    counts = [jnp.int32(0)] * tiles_dev
    for b, row in enumerate(stored):
        for slot in row:
            tile = slot - owner * tiles_dev
            block = jnp.where((tile >= 0) & (tile < tiles_dev), jnp.int32(b), block)
            counts = [n + (tile == i).astype(jnp.int32) for i, n in enumerate(counts)]
    return block, counts


def owner_at(where_ref, distance, ctx_count):
    return lax.rem(where_ref[0] + distance, ctx_count)


def pack_body(where_ref, pairs_ref, slots_ref, q_ref, kv_hbm, *refs, tiles_dev, kv_used):
    out_refs, sem = refs[:-1], refs[-1]
    ctx_count = len(out_refs)
    heads = q_ref.shape[1] // HEAD_DIM
    tok_rows = kv_hbm.shape[1]
    kv_at = heads * BLOCK + META_ROWS
    copies = []
    for w in range(2):
        for k in range(kv_used):
            cols = pl.ds(pl.multiple_of((where_ref[1] + k) * HEAD_DIM, HEAD_DIM), HEAD_DIM)
            part = w * kv_used + k
            rows = pl.ds(kv_at + part * tok_rows, tok_rows)
            copies.append(
                pltpu.make_async_copy(kv_hbm.at[w, :, cols], out_refs[1].at[rows, :], sem.at[part])
            )
    for copy in copies:
        copy.start()
    stored = owner_slots(pairs_ref, slots_ref)
    lanes = lax.broadcasted_iota(jnp.int32, (META_ROWS, HEAD_DIM), 1)
    for distance, out_ref in enumerate(out_refs):
        block, counts = block_for(stored, owner_at(where_ref, distance, ctx_count), tiles_dev)
        rows = pl.ds(pl.multiple_of(block * BLOCK, BLOCK), BLOCK)
        for h in range(heads):
            out_ref[h * BLOCK : (h + 1) * BLOCK, :] = q_ref[rows, h * HEAD_DIM : (h + 1) * HEAD_DIM]
        meta = jnp.zeros((META_ROWS, HEAD_DIM), jnp.float32)
        for i, n in enumerate(counts):
            meta = jnp.where(lanes % tiles_dev == i, n.astype(jnp.float32), meta)
        out_ref[heads * BLOCK : kv_at, :] = meta.astype(jnp.bfloat16)
    for copy in copies:
        copy.wait()


def pack_queries(where, pair_tiles, tile_slot, q_cross, kv_self, ctx_count, tiles_dev, kv_used):
    rows = q_cross.shape[1] // HEAD_DIM * BLOCK + META_ROWS
    kv_rows = 2 * kv_used * kv_self.shape[1]
    return pl.pallas_call(
        functools.partial(pack_body, tiles_dev=tiles_dev, kv_used=kv_used),
        out_shape=[
            pltpu.VMEM((rows + (kv_rows if d == 1 else 0), HEAD_DIM), jnp.bfloat16)
            for d in range(ctx_count)
        ],
        in_specs=[SMEM, SMEM, SMEM, VMEM, ANY],
        out_specs=[VMEM] * ctx_count,
        scratch_shapes=[pltpu.SemaphoreType.DMA((2 * kv_used,))],
        compiler_params=PARAMS,
        name="pack_queries",
    )(where, pair_tiles, tile_slot, q_cross, kv_self)


def attend_head(q, meta, keys, values, key_count, scores_sc):
    rows = q.shape[0]
    padded = keys.shape[0]
    lanes = HEAD_DIM
    count = meta[0:1, :].astype(jnp.float32)
    bias = jnp.where(count > 0, jnp.log(jnp.maximum(count, 1.0)) * LOG2E, NEG_FILL)
    best = None
    for at in range(0, padded, KEY_CHUNK):
        size = min(KEY_CHUNK, padded - at)
        scores = lax.dot_general(
            q, keys[at : at + size, :], (((1,), (1,)), ((), ())), preferred_element_type=jnp.float32
        )
        for col in range(0, size, lanes):
            width = min(lanes, size - col)
            piece = scores[:, col : col + width]
            valid = key_count - at - col
            if width > valid:
                piece = jnp.where(lax.broadcasted_iota(jnp.int32, piece.shape, 1) < valid, piece, NEG_FILL)
            scores_sc[:, at + col : at + col + width] = piece
            if width == lanes:
                best = piece if best is None else jnp.maximum(best, piece)
            else:
                tail = piece
    best = jnp.max(best * EXP2_SCALE + bias, axis=1, keepdims=True)
    tail_width = padded % lanes
    if tail_width:
        tail = jnp.max(tail * EXP2_SCALE + bias[:, :tail_width], axis=1, keepdims=True)
        best = jnp.maximum(best, tail)
    shift = jnp.where(best > 0.5 * NEG_FILL, bias - best, NEG_FILL)
    totals = jnp.zeros((rows, lanes), jnp.float32)
    total = jnp.zeros((rows, 1), jnp.float32)
    blended = jnp.zeros((rows, HEAD_DIM), jnp.float32)
    for at in range(0, padded, KEY_CHUNK):
        size = min(KEY_CHUNK, padded - at)
        pieces = []
        for col in range(0, size, lanes):
            width = min(lanes, size - col)
            piece = scores_sc[:, at + col : at + col + width]
            weights = jnp.exp2(piece * EXP2_SCALE + shift[:, :width])
            if width == lanes:
                totals = totals + weights
            else:
                total = total + jnp.sum(weights, axis=1, keepdims=True)
            pieces.append(weights.astype(jnp.bfloat16))
        weights = jnp.concatenate(pieces, axis=1) if len(pieces) > 1 else pieces[0]
        blended = blended + jnp.dot(
            weights, values[at : at + size, :], preferred_element_type=jnp.float32
        )
    total = total + jnp.sum(totals, axis=1, keepdims=True)
    live = total > 0
    total = jnp.where(live, total, 1.0)
    out = (blended / total).astype(jnp.bfloat16)
    lse = jnp.where(live, best * (1.0 / LOG2E) + jnp.log(total), NEG_FILL)
    return out, jnp.broadcast_to(lse, (rows, lanes))


def attend_block(q_ref, keys_ref, values_ref, out_ref, lse_ref, scores_sc, key_count, wait):
    kv_used, padded_len, tiles_dev, _ = keys_ref.shape
    padded = padded_len * tiles_dev
    q_rows = scores_sc.shape[0] * kv_used
    rows = scores_sc.shape[0]
    meta = q_ref[q_rows : q_rows + META_ROWS, :]
    for k in range(kv_used):
        wait(k)
        own = slice(k * rows, (k + 1) * rows)
        keys = keys_ref.at[k].reshape(padded, HEAD_DIM)
        values = values_ref.at[k].reshape(padded, HEAD_DIM)
        out, lse = attend_head(q_ref[own, :], meta, keys, values, key_count, scores_sc)
        out_ref[own, :] = out
        if lse_ref is not None:
            lse_ref[own, :] = lse


def own_body(where_ref, q_ref, image_hbm, *refs, with_lse):
    out_ref = refs[0]
    lse_ref = refs[1] if with_lse else None
    keys_ref, values_ref, scores_sc, sem = refs[-4:]
    tile_len, tiles_dev = image_hbm.shape[1:3]
    kv_used, padded_len = keys_ref.shape[:2]

    def copies(k):
        cols = pl.ds(pl.multiple_of((where_ref[1] + k) * HEAD_DIM, HEAD_DIM), HEAD_DIM)
        held = pl.ds(0, tile_len)
        return [
            pltpu.make_async_copy(image_hbm.at[w, :, :, cols], ref.at[k, held], sem.at[w, k])
            for w, ref in enumerate((keys_ref, values_ref))
        ]

    for k in range(kv_used):
        for copy in copies(k):
            copy.start()
    pad = jnp.zeros((padded_len - tile_len, tiles_dev, HEAD_DIM), jnp.bfloat16)
    for k in range(kv_used):
        keys_ref[k, tile_len:] = pad
        values_ref[k, tile_len:] = pad

    def wait(k):
        for copy in copies(k):
            copy.wait()

    attend_block(
        q_ref, keys_ref, values_ref, out_ref, lse_ref, scores_sc, tile_len * tiles_dev, wait
    )


def attend_own(where, packed, image_kv, kv_used, q_rows, with_lse):
    _, tile_len, tiles_dev, _ = image_kv.shape
    held = pltpu.VMEM((kv_used, -(-tile_len // 8) * 8, tiles_dev, HEAD_DIM), jnp.bfloat16)
    out_shape = [pltpu.VMEM((q_rows, HEAD_DIM), jnp.bfloat16)]
    if with_lse:
        out_shape.append(pltpu.VMEM((q_rows, HEAD_DIM), jnp.float32))
    out_shape += [held, held]
    padded = held.shape[1] * tiles_dev
    results = pl.pallas_call(
        functools.partial(own_body, with_lse=with_lse),
        out_shape=out_shape,
        in_specs=[SMEM, VMEM, ANY],
        out_specs=[VMEM] * len(out_shape),
        scratch_shapes=[
            pltpu.VMEM((q_rows // kv_used, padded), jnp.float32),
            pltpu.SemaphoreType.DMA((2, kv_used)),
        ],
        compiler_params=PARAMS,
        name="attend_own",
    )(where, in_vmem(packed), image_kv)
    return results[:-2], [in_vmem(part) for part in results[-2:]]


def arrived_body(q_ref, keys_ref, values_ref, *refs, with_lse, riders, key_count, q_rows):
    rider_refs, refs = refs[: len(riders)], refs[len(riders) :]
    out_ref, scores_sc = refs[0], refs[-1]
    lse_ref = refs[1] if with_lse else None
    for ref, at in zip(rider_refs, riders):
        out_ref[q_rows:, :] = ref[at:, :]
    attend_block(
        q_ref, keys_ref, values_ref, out_ref, lse_ref, scores_sc, key_count, lambda k: None
    )


def attend_arrived(packed, held, key_count, q_rows, with_lse, rider=None):
    kv_used, padded_len, tiles_dev, _ = held[0].shape
    at = q_rows + META_ROWS
    riders = [] if rider is None else [rider]
    extra = 0 if rider is None else rider.shape[0] - at
    out_shape = [pltpu.VMEM((q_rows + extra, HEAD_DIM), jnp.bfloat16)]
    if with_lse:
        out_shape.append(pltpu.VMEM((q_rows, HEAD_DIM), jnp.float32))
    return pl.pallas_call(
        functools.partial(
            arrived_body,
            with_lse=with_lse,
            riders=[at] * len(riders),
            key_count=key_count,
            q_rows=q_rows,
        ),
        out_shape=out_shape,
        in_specs=[VMEM] * (3 + len(riders)),
        out_specs=[VMEM] * len(out_shape),
        scratch_shapes=[pltpu.VMEM((q_rows // kv_used, padded_len * tiles_dev), jnp.float32)],
        compiler_params=PARAMS,
        name="attend_arrived",
    )(in_vmem(packed), *held, *riders)


def self_body(where_ref, docs_ref, q_ref, *refs, starts, kv_used):
    kv_refs, out_ref, bias_sc = refs[:-2], refs[-2], refs[-1]
    tok_rows, q_width = q_ref.shape
    per_kv = q_width // HEAD_DIM // kv_used
    shape = bias_sc.shape
    row_start = where_ref[0] * tok_rows
    query_pos = row_start + lax.broadcasted_iota(jnp.int32, (tok_rows, 1), 0)
    key_pos = row_start + tok_rows - shape[1] + lax.broadcasted_iota(jnp.int32, shape, 1)
    doc_start = jnp.zeros((tok_rows, 1), jnp.int32)
    doc_end = jnp.int32(0)
    for j in range(docs_ref.shape[0]):
        doc_end = doc_end + docs_ref[j]
        doc_start = jnp.where(query_pos >= doc_end, doc_end, doc_start)
    bias_sc[...] = jnp.where((key_pos <= query_pos) & (key_pos >= doc_start), 0.0, NEG_FILL)
    for k in range(kv_used):
        keys, values = [
            jnp.concatenate(
                [
                    ref[at + (w * kv_used + k) * tok_rows : at + (w * kv_used + k + 1) * tok_rows, :]
                    for ref, at in zip(kv_refs, starts)
                ],
                axis=0,
            )
            for w in range(2)
        ]
        heads = range(k * per_kv, (k + 1) * per_kv)
        q = jnp.concatenate([q_ref[:, h * HEAD_DIM : (h + 1) * HEAD_DIM] for h in heads], axis=0)
        scores = lax.dot_general(
            q, keys, (((1,), (1,)), ((), ())), preferred_element_type=jnp.float32
        )
        scores = scores * EXP2_SCALE + jnp.concatenate([bias_sc[...]] * per_kv, axis=0)
        row_best = jnp.max(scores, axis=1, keepdims=True)
        weights = jnp.exp2(scores - row_best)
        row_total = jnp.sum(weights, axis=1, keepdims=True)
        blended = jnp.dot(weights.astype(jnp.bfloat16), values, preferred_element_type=jnp.float32)
        blended = blended / row_total
        for i, h in enumerate(heads):
            out_ref[:, h * HEAD_DIM : (h + 1) * HEAD_DIM] = blended[i * tok_rows : (i + 1) * tok_rows]


def attend_self(where, doc_lengths, q_self, pieces, kv_used):
    tok_rows, q_width = q_self.shape
    return pl.pallas_call(
        functools.partial(self_body, starts=[at for _, at in pieces], kv_used=kv_used),
        out_shape=pltpu.VMEM((tok_rows, q_width), jnp.float32),
        in_specs=[SMEM, SMEM] + [VMEM] * (1 + len(pieces)),
        out_specs=VMEM,
        scratch_shapes=[pltpu.VMEM((tok_rows, len(pieces) * tok_rows), jnp.float32)],
        compiler_params=PARAMS,
        name="attend_self",
    )(where, doc_lengths, in_vmem(q_self), *[in_vmem(array) for array, _ in pieces])


def mix_body(where_ref, pairs_ref, slots_ref, gate_ref, self_ref, *refs, tiles_dev):
    partial_refs, out_ref = refs[:-1], refs[-1]
    stored = owner_slots(pairs_ref, slots_ref)
    for distance, partial_ref in enumerate(partial_refs):
        owner = owner_at(where_ref, distance, len(partial_refs))
        block, _ = block_for(stored, owner, tiles_dev)
        rows = pl.ds(pl.multiple_of(block * BLOCK, BLOCK), BLOCK)
        for h in range(self_ref.shape[1] // HEAD_DIM):
            cols = slice(h * HEAD_DIM, (h + 1) * HEAD_DIM)
            cross = partial_ref[h * BLOCK : (h + 1) * BLOCK, :].astype(jnp.float32)
            mixed = self_ref[rows, cols] + gate_ref[:, cols] * cross
            out_ref[rows, cols] = mixed.astype(jnp.bfloat16)


def mix(where, pair_tiles, tile_slot, gate_cols, self_out, partials, tiles_dev):
    return pl.pallas_call(
        functools.partial(mix_body, tiles_dev=tiles_dev),
        out_shape=jax.ShapeDtypeStruct(self_out.shape, jnp.bfloat16),
        in_specs=[SMEM] * 3 + [VMEM] * (2 + len(partials)),
        out_specs=VMEM,
        compiler_params=PARAMS,
        name="mix",
    )(
        where,
        pair_tiles,
        tile_slot,
        gate_cols,
        in_vmem(self_out),
        *[in_vmem(partial) for partial in partials],
    )


def mix_owners(where, pair_tiles, tile_slot, gate_cols, self_out, partials, sums, tiles_dev):
    block_count = pair_tiles.shape[0]
    tok_rows, q_width = self_out.shape
    heads = q_width // HEAD_DIM
    ctx_count = len(partials)
    owners = jnp.take(tile_slot, pair_tiles.reshape(-1), axis=0).reshape(block_count, -1) // tiles_dev
    partners = (where[0] + jnp.arange(ctx_count, dtype=jnp.int32)) % ctx_count
    live = jnp.any(owners[:, :, None] == partners[None, None, :], axis=1)[:, :, None, None]
    lse = jnp.stack(sums)[None]
    top = jnp.max(jnp.where(live, lse, NEG_FILL), axis=1, keepdims=True)
    factors = jnp.where(live, jnp.exp(lse - top), 0.0)
    pieces = jnp.stack(partials).astype(jnp.float32)[None]
    cross = jnp.sum(factors * pieces, axis=1) / jnp.sum(factors, axis=1)
    cross = jnp.transpose(cross.reshape(block_count, heads, BLOCK, HEAD_DIM), (0, 2, 1, 3))
    return (self_out + gate_cols * cross.reshape(tok_rows, q_width)).astype(jnp.bfloat16)


def local(q_self, q_cross, kv_self, image_kv, cross_gate, doc_lengths, pair_tiles, tile_slot):
    tok_rows, q_width = q_self.shape
    local_heads = q_width // HEAD_DIM
    q_rows = local_heads * BLOCK
    grouping = Q_HEADS // KV_HEADS
    per_kv = min(local_heads, grouping)
    kv_used = local_heads // per_kv
    ctx_count = lax.axis_size("ctx")
    tiles_dev, tile_len = image_kv.shape[1:3]
    request_count = pair_tiles.shape[0] * PAIRS
    capacity = max(2, -(-request_count // ctx_count))
    one_owner = ctx_count * capacity == request_count and capacity == PAIRS
    with_lse = not one_owner
    reach = min(ctx_count - 1, -(-(ctx_count * tok_rows // 2 - 1) // tok_rows))

    here = lax.axis_index("ctx").astype(jnp.int32)
    kv_first = (lax.axis_index("rep") * local_heads // grouping).astype(jnp.int32)
    where = jnp.stack([here, kv_first])
    image_kv = jnp.transpose(image_kv, (0, 2, 1, 3))

    def send(array, distance):
        pairs = [(i, (i + distance) % ctx_count) for i in range(ctx_count)]
        return lax.ppermute(array, "ctx", pairs)

    packed = pack_queries(
        where, pair_tiles, tile_slot, q_cross, kv_self, ctx_count, tiles_dev, kv_used
    )
    last = ctx_count - 1
    order = [last] + list(range(last - 1, 0, -1))
    arrived = {d: send(packed[d], d) for d in [1] + order[:-1]}
    results = {}
    results[0], held = attend_own(where, packed[0], image_kv, kv_used, q_rows, with_lse)
    for d in order:
        rider = in_vmem(arrived[1]) if d == last else None
        answer = attend_arrived(
            arrived[d], held, tile_len * tiles_dev, q_rows, with_lse, rider
        )
        results[d] = [send(part, ctx_count - d) for part in answer]

    at = q_rows + META_ROWS
    pieces = [(packed[1], at), (arrived[1], at), (results[last][0], q_rows)][: reach + 1]
    for _ in range(len(pieces), reach + 1):
        array, first = pieces[-1]
        pieces.append((send(array[first:], 1), 0))
    self_out = attend_self(where, doc_lengths, q_self, pieces[::-1], kv_used)
    gate_cols = jnp.repeat(jnp.tanh(cross_gate), HEAD_DIM)[None, :]
    partials = [results[d][0] for d in range(ctx_count)]
    if one_owner:
        return mix(where, pair_tiles, tile_slot, gate_cols, self_out, partials, tiles_dev)
    partials = [partial[:q_rows] for partial in partials]
    sums = [results[d][1] for d in range(ctx_count)]
    return mix_owners(where, pair_tiles, tile_slot, gate_cols, self_out, partials, sums, tiles_dev)


def solution(mesh):
    in_specs = (
        P(("groups", "ctx"), ("head", "rep")),
        P(("groups", "ctx"), ("head", "rep")),
        P(None, ("groups", "ctx"), "head"),
        P(None, ("groups", "ctx"), None, "head"),
        P(("head", "rep")),
        P("groups"),
        P(("groups", "ctx"), None),
        P("groups"),
    )
    out_specs = P(("groups", "ctx"), ("head", "rep"))
    return jax.shard_map(local, mesh=mesh, in_specs=in_specs, out_specs=out_specs, check_vma=False)
```

```python
import functools
import math

import jax
import jax.numpy as jnp
from jax import lax
from jax.experimental import pallas as pl
from jax.experimental.pallas import tpu as pltpu
from jax.sharding import PartitionSpec as P


HEAD_DIM = 128
Q_HEADS = 64
KV_HEADS = 8
BLOCK = 32
PAIRS = 4

NEG_FILL = -1e30
META_ROWS = 8
KEY_CHUNK = 256
LOG2E = math.log2(math.e)
EXP2_SCALE = HEAD_DIM ** (-0.5) * LOG2E

SMEM = pl.BlockSpec(memory_space=pltpu.SMEM)
VMEM = pl.BlockSpec(memory_space=pltpu.VMEM)
HBM = pl.BlockSpec(memory_space=pltpu.HBM)
PARAMS = pltpu.CompilerParams(vmem_limit_bytes=24 << 20)


def in_vmem(array):
    return pltpu.with_memory_space_constraint(array, pltpu.VMEM)


def in_hbm(array):
    return pltpu.with_memory_space_constraint(array, pltpu.HBM)


def owner_slots(pairs_ref, slots_ref):
    blocks, pairs = pairs_ref.shape
    return [[slots_ref[pairs_ref[b, p]] for p in range(pairs)] for b in range(blocks)]


def block_for(stored, owner, tiles_dev):
    block = jnp.int32(0)
    counts = [jnp.int32(0)] * tiles_dev
    for b, row in enumerate(stored):
        for slot in row:
            tile = slot - owner * tiles_dev
            block = jnp.where((tile >= 0) & (tile < tiles_dev), jnp.int32(b), block)
            counts = [n + (tile == i).astype(jnp.int32) for i, n in enumerate(counts)]
    return block, counts


def owner_at(where_ref, distance, ctx_count):
    return lax.rem(where_ref[0] + distance, ctx_count)


def pack_body(where_ref, pairs_ref, slots_ref, q_ref, kv_hbm, *refs, tiles_dev, kv_used):
    out_refs, sem = refs[:-1], refs[-1]
    ctx_count = len(out_refs)
    heads = q_ref.shape[1] // HEAD_DIM
    tok_rows = kv_hbm.shape[1]
    kv_at = heads * BLOCK
    copies = []
    for w in range(2):
        for k in range(kv_used):
            cols = pl.ds(pl.multiple_of((where_ref[1] + k) * HEAD_DIM, HEAD_DIM), HEAD_DIM)
            part = w * kv_used + k
            rows = pl.ds(kv_at + part * tok_rows, tok_rows)
            copies.append(
                pltpu.make_async_copy(kv_hbm.at[w, :, cols], out_refs[1].at[rows, :], sem.at[part])
            )
    for copy in copies:
        copy.start()
    stored = owner_slots(pairs_ref, slots_ref)
    lanes = lax.broadcasted_iota(jnp.int32, (META_ROWS, HEAD_DIM), 1)
    for distance, out_ref in enumerate(out_refs):
        block, counts = block_for(stored, owner_at(where_ref, distance, ctx_count), tiles_dev)
        rows = pl.ds(pl.multiple_of(block * BLOCK, BLOCK), BLOCK)
        for h in range(heads):
            out_ref[h * BLOCK : (h + 1) * BLOCK, :] = q_ref[rows, h * HEAD_DIM : (h + 1) * HEAD_DIM]
        meta = jnp.zeros((META_ROWS, HEAD_DIM), jnp.float32)
        for i, n in enumerate(counts):
            meta = jnp.where(lanes % tiles_dev == i, n.astype(jnp.float32), meta)
        out_ref[out_ref.shape[0] - META_ROWS :, :] = meta.astype(jnp.bfloat16)
    for copy in copies:
        copy.wait()


def pack_queries(where, pair_tiles, tile_slot, q_cross, kv_self, ctx_count, tiles_dev, kv_used):
    rows = q_cross.shape[1] // HEAD_DIM * BLOCK + META_ROWS
    kv_rows = 2 * kv_used * kv_self.shape[1]
    return pl.pallas_call(
        functools.partial(pack_body, tiles_dev=tiles_dev, kv_used=kv_used),
        out_shape=[
            pltpu.VMEM((rows + (kv_rows if d == 1 else 0), HEAD_DIM), jnp.bfloat16)
            for d in range(ctx_count)
        ],
        in_specs=[SMEM, SMEM, SMEM, VMEM, HBM],
        out_specs=[VMEM] * ctx_count,
        scratch_shapes=[pltpu.SemaphoreType.DMA((2 * kv_used,))],
        compiler_params=PARAMS,
        name="pack_queries",
    )(where, in_hbm(pair_tiles), in_hbm(tile_slot), in_hbm(q_cross), in_hbm(kv_self))


def attend_head(q, meta, keys, values, key_count, scores_sc, wait_values):
    rows = q.shape[0]
    padded = keys.shape[0]
    lanes = HEAD_DIM
    count = meta[0:1, :].astype(jnp.float32)
    bias = jnp.where(count > 0, jnp.log(jnp.maximum(count, 1.0)) * LOG2E, NEG_FILL)
    best = None
    for at in range(0, padded, KEY_CHUNK):
        size = min(KEY_CHUNK, padded - at)
        scores = lax.dot_general(
            q, keys[at : at + size, :], (((1,), (1,)), ((), ())), preferred_element_type=jnp.float32
        )
        for col in range(0, size, lanes):
            width = min(lanes, size - col)
            piece = scores[:, col : col + width]
            valid = key_count - at - col
            if width > valid:
                piece = jnp.where(lax.broadcasted_iota(jnp.int32, piece.shape, 1) < valid, piece, NEG_FILL)
            scores_sc[:, at + col : at + col + width] = piece
            if width == lanes:
                best = piece if best is None else jnp.maximum(best, piece)
            else:
                tail = piece
    best = jnp.max(best * EXP2_SCALE + bias, axis=1, keepdims=True)
    tail_width = padded % lanes
    if tail_width:
        tail = jnp.max(tail * EXP2_SCALE + bias[:, :tail_width], axis=1, keepdims=True)
        best = jnp.maximum(best, tail)
    wait_values()
    shift = jnp.where(best > 0.5 * NEG_FILL, bias - best, NEG_FILL)
    totals = jnp.zeros((rows, lanes), jnp.float32)
    total = jnp.zeros((rows, 1), jnp.float32)
    blended = jnp.zeros((rows, HEAD_DIM), jnp.float32)
    for at in range(0, padded, KEY_CHUNK):
        size = min(KEY_CHUNK, padded - at)
        pieces = []
        for col in range(0, size, lanes):
            width = min(lanes, size - col)
            piece = scores_sc[:, at + col : at + col + width]
            weights = jnp.exp2(piece * EXP2_SCALE + shift[:, :width])
            if width == lanes:
                totals = totals + weights
            else:
                total = total + jnp.sum(weights, axis=1, keepdims=True)
            pieces.append(weights.astype(jnp.bfloat16))
        weights = jnp.concatenate(pieces, axis=1) if len(pieces) > 1 else pieces[0]
        blended = blended + jnp.dot(
            weights, values[at : at + size, :], preferred_element_type=jnp.float32
        )
    total = total + jnp.sum(totals, axis=1, keepdims=True)
    live = total > 0
    total = jnp.where(live, total, 1.0)
    out = (blended / total).astype(jnp.bfloat16)
    lse = jnp.where(live, best * (1.0 / LOG2E) + jnp.log(total), NEG_FILL)
    return out, jnp.broadcast_to(lse, (rows, lanes))


def attend_block(q_ref, keys_ref, values_ref, out_ref, lse_ref, scores_sc, key_count, wait):
    kv_used = keys_ref.shape[0]
    rows = scores_sc.shape[0]
    meta = q_ref[q_ref.shape[0] - META_ROWS :, :]
    for k in range(kv_used):
        wait_values = wait(k)
        own = slice(k * rows, (k + 1) * rows)
        keys, values = keys_ref.at[k], values_ref.at[k]
        out, lse = attend_head(q_ref[own, :], meta, keys, values, key_count, scores_sc, wait_values)
        out_ref[own, :] = out
        if lse_ref is not None:
            lse_ref[own, :] = lse


def no_wait(k):
    return lambda: None


def own_body(where_ref, q_ref, image_hbm, *refs, with_lse):
    out_ref = refs[0]
    lse_ref = refs[1] if with_lse else None
    keys_ref, values_ref, scores_sc, sem = refs[-4:]
    _, tile_len, tiles_dev, width = image_hbm.shape
    key_count = tile_len * tiles_dev
    kv_used, padded = keys_ref.shape[:2]
    image = image_hbm.reshape(2, key_count, width)

    def copies(k):
        cols = pl.ds(pl.multiple_of((where_ref[1] + k) * HEAD_DIM, HEAD_DIM), HEAD_DIM)
        held = pl.ds(0, key_count)
        return [
            pltpu.make_async_copy(image.at[w, :, cols], ref.at[k, held], sem.at[w, k])
            for w, ref in enumerate((keys_ref, values_ref))
        ]

    for copy in copies(0):
        copy.start()
    if padded > key_count:
        pad = jnp.zeros((padded - key_count, HEAD_DIM), jnp.bfloat16)
        for k in range(kv_used):
            keys_ref[k, key_count:, :] = pad
            values_ref[k, key_count:, :] = pad

    def wait(k):
        keys, values = copies(k)
        keys.wait()
        if k == 0:
            for later in range(1, kv_used):
                for copy in copies(later):
                    copy.start()
        return values.wait

    attend_block(
        q_ref, keys_ref, values_ref, out_ref, lse_ref, scores_sc, key_count, wait
    )


def attend_own(where, packed, image_kv, kv_used, q_rows, with_lse):
    _, tile_len, tiles_dev, _ = image_kv.shape
    padded = -(-tile_len * tiles_dev // 16) * 16
    held = pltpu.VMEM((kv_used, padded, HEAD_DIM), jnp.bfloat16)
    out_shape = [pltpu.VMEM((q_rows, HEAD_DIM), jnp.bfloat16)]
    if with_lse:
        out_shape.append(pltpu.VMEM((q_rows, HEAD_DIM), jnp.float32))
    out_shape += [held, held]
    results = pl.pallas_call(
        functools.partial(own_body, with_lse=with_lse),
        out_shape=out_shape,
        in_specs=[SMEM, VMEM, HBM],
        out_specs=[VMEM] * len(out_shape),
        scratch_shapes=[
            pltpu.VMEM((q_rows // kv_used, padded), jnp.float32),
            pltpu.SemaphoreType.DMA((2, kv_used)),
        ],
        compiler_params=PARAMS,
        name="attend_own",
    )(where, in_vmem(packed), in_hbm(image_kv))
    return results[:-2], [in_vmem(part) for part in results[-2:]]


def arrived_body(q_ref, keys_ref, values_ref, *refs, with_lse, riders, key_count, q_rows):
    rider_refs, refs = refs[:riders], refs[riders:]
    out_ref, scores_sc = refs[0], refs[-1]
    lse_ref = refs[1] if with_lse else None
    for ref in rider_refs:
        out_ref[q_rows:, :] = ref[q_rows : out_ref.shape[0], :]
    attend_block(
        q_ref, keys_ref, values_ref, out_ref, lse_ref, scores_sc, key_count, no_wait
    )


def attend_arrived(packed, held, key_count, q_rows, with_lse, rider=None):
    kv_used, padded, _ = held[0].shape
    riders = [] if rider is None else [rider]
    extra = 0 if rider is None else rider.shape[0] - q_rows - META_ROWS
    out_shape = [pltpu.VMEM((q_rows + extra, HEAD_DIM), jnp.bfloat16)]
    if with_lse:
        out_shape.append(pltpu.VMEM((q_rows, HEAD_DIM), jnp.float32))
    return pl.pallas_call(
        functools.partial(
            arrived_body,
            with_lse=with_lse,
            riders=len(riders),
            key_count=key_count,
            q_rows=q_rows,
        ),
        out_shape=out_shape,
        in_specs=[VMEM] * (3 + len(riders)),
        out_specs=[VMEM] * len(out_shape),
        scratch_shapes=[pltpu.VMEM((q_rows // kv_used, padded), jnp.float32)],
        compiler_params=PARAMS,
        name="attend_arrived",
    )(in_vmem(packed), *held, *riders)


def self_body(where_ref, docs_ref, q_ref, *refs, starts, kv_used):
    kv_refs, out_ref, bias_sc = refs[:-2], refs[-2], refs[-1]
    tok_rows, q_width = q_ref.shape
    per_kv = q_width // HEAD_DIM // kv_used
    shape = bias_sc.shape
    row_start = where_ref[0] * tok_rows
    query_pos = row_start + lax.broadcasted_iota(jnp.int32, (tok_rows, 1), 0)
    key_pos = row_start + tok_rows - shape[1] + lax.broadcasted_iota(jnp.int32, shape, 1)
    doc_start = jnp.zeros((tok_rows, 1), jnp.int32)
    doc_end = jnp.int32(0)
    for j in range(docs_ref.shape[0]):
        doc_end = doc_end + docs_ref[j]
        doc_start = jnp.where(query_pos >= doc_end, doc_end, doc_start)
    bias_sc[...] = jnp.where((key_pos <= query_pos) & (key_pos >= doc_start), 0.0, NEG_FILL)
    for k in range(kv_used):
        keys, values = [
            jnp.concatenate(
                [
                    ref[at + (w * kv_used + k) * tok_rows : at + (w * kv_used + k + 1) * tok_rows, :]
                    for ref, at in zip(kv_refs, starts)
                ],
                axis=0,
            )
            for w in range(2)
        ]
        heads = range(k * per_kv, (k + 1) * per_kv)
        q = jnp.concatenate([q_ref[:, h * HEAD_DIM : (h + 1) * HEAD_DIM] for h in heads], axis=0)
        scores = lax.dot_general(
            q, keys, (((1,), (1,)), ((), ())), preferred_element_type=jnp.float32
        )
        scores = scores * EXP2_SCALE + jnp.concatenate([bias_sc[...]] * per_kv, axis=0)
        row_best = jnp.max(scores, axis=1, keepdims=True)
        weights = jnp.exp2(scores - row_best)
        row_total = jnp.sum(weights, axis=1, keepdims=True)
        blended = jnp.dot(weights.astype(jnp.bfloat16), values, preferred_element_type=jnp.float32)
        blended = blended / row_total
        for i, h in enumerate(heads):
            out_ref[:, h * HEAD_DIM : (h + 1) * HEAD_DIM] = blended[i * tok_rows : (i + 1) * tok_rows]


def attend_self(where, doc_lengths, q_self, pieces, kv_used):
    tok_rows, q_width = q_self.shape
    return pl.pallas_call(
        functools.partial(self_body, starts=[at for _, at in pieces], kv_used=kv_used),
        out_shape=pltpu.VMEM((tok_rows, q_width), jnp.float32),
        in_specs=[SMEM, SMEM] + [VMEM] * (1 + len(pieces)),
        out_specs=VMEM,
        scratch_shapes=[pltpu.VMEM((tok_rows, len(pieces) * tok_rows), jnp.float32)],
        compiler_params=PARAMS,
        name="attend_self",
    )(where, doc_lengths, in_vmem(q_self), *[in_vmem(array) for array, _ in pieces])


def mix_body(where_ref, pairs_ref, slots_ref, gate_ref, self_ref, *refs, tiles_dev):
    partial_refs, out_ref = refs[:-1], refs[-1]
    stored = owner_slots(pairs_ref, slots_ref)
    for distance, partial_ref in enumerate(partial_refs):
        owner = owner_at(where_ref, distance, len(partial_refs))
        block, _ = block_for(stored, owner, tiles_dev)
        rows = pl.ds(pl.multiple_of(block * BLOCK, BLOCK), BLOCK)
        for h in range(self_ref.shape[1] // HEAD_DIM):
            cols = slice(h * HEAD_DIM, (h + 1) * HEAD_DIM)
            cross = partial_ref[h * BLOCK : (h + 1) * BLOCK, :].astype(jnp.float32)
            mixed = self_ref[rows, cols] + gate_ref[:, cols] * cross
            out_ref[rows, cols] = mixed.astype(jnp.bfloat16)


def mix(where, pair_tiles, tile_slot, gate_cols, self_out, partials, tiles_dev):
    return pl.pallas_call(
        functools.partial(mix_body, tiles_dev=tiles_dev),
        out_shape=jax.ShapeDtypeStruct(self_out.shape, jnp.bfloat16),
        in_specs=[SMEM] * 3 + [VMEM] * (2 + len(partials)),
        out_specs=VMEM,
        compiler_params=PARAMS,
        name="mix",
    )(
        where,
        pair_tiles,
        tile_slot,
        gate_cols,
        in_vmem(self_out),
        *[in_vmem(partial) for partial in partials],
    )


def mix_owners(where, pair_tiles, tile_slot, gate_cols, self_out, partials, sums, tiles_dev):
    block_count = pair_tiles.shape[0]
    tok_rows, q_width = self_out.shape
    heads = q_width // HEAD_DIM
    ctx_count = len(partials)
    owners = jnp.take(tile_slot, pair_tiles.reshape(-1), axis=0).reshape(block_count, -1) // tiles_dev
    partners = (where[0] + jnp.arange(ctx_count, dtype=jnp.int32)) % ctx_count
    live = jnp.any(owners[:, :, None] == partners[None, None, :], axis=1)[:, :, None, None]
    lse = jnp.stack(sums)[None]
    top = jnp.max(jnp.where(live, lse, NEG_FILL), axis=1, keepdims=True)
    factors = jnp.where(live, jnp.exp(lse - top), 0.0)
    pieces = jnp.stack(partials).astype(jnp.float32)[None]
    cross = jnp.sum(factors * pieces, axis=1) / jnp.sum(factors, axis=1)
    cross = jnp.transpose(cross.reshape(block_count, heads, BLOCK, HEAD_DIM), (0, 2, 1, 3))
    return (self_out + gate_cols * cross.reshape(tok_rows, q_width)).astype(jnp.bfloat16)


def partner_order(ctx_count):
    return list(range(ctx_count - 1, 0, -1))


def attend(q_self, q_cross, kv_self, image_kv, cross_gate, doc_lengths, pair_tiles, tile_slot):
    tok_rows, q_width = q_self.shape
    local_heads = q_width // HEAD_DIM
    q_rows = local_heads * BLOCK
    grouping = Q_HEADS // KV_HEADS
    per_kv = min(local_heads, grouping)
    kv_used = local_heads // per_kv
    ctx_count = lax.axis_size("ctx")
    tiles_dev, tile_len = image_kv.shape[1:3]
    request_count = pair_tiles.shape[0] * PAIRS
    capacity = max(2, -(-request_count // ctx_count))
    one_owner = ctx_count * capacity == request_count and capacity == PAIRS
    with_lse = not one_owner
    reach = min(ctx_count - 1, -(-(ctx_count * tok_rows // 2 - 1) // tok_rows))

    here = lax.axis_index("ctx").astype(jnp.int32)
    kv_first = (lax.axis_index("rep") * local_heads // grouping).astype(jnp.int32)
    where = jnp.stack([here, kv_first])
    image_kv = jnp.transpose(image_kv, (0, 2, 1, 3))

    def send(array, distance):
        pairs = [(i, (i + distance) % ctx_count) for i in range(ctx_count)]
        return lax.ppermute(array, "ctx", pairs)

    packed = pack_queries(
        where, pair_tiles, tile_slot, q_cross, kv_self, ctx_count, tiles_dev, kv_used
    )
    last = ctx_count - 1
    order = partner_order(ctx_count)
    arrived = {d: send(packed[d], d) for d in order[-1:] + order[:-1]}
    results = {}
    results[0], held = attend_own(where, packed[0], image_kv, kv_used, q_rows, with_lse)
    for d in order:
        rider = in_vmem(arrived[1]) if d == last else None
        answer = attend_arrived(
            arrived[d], held, tile_len * tiles_dev, q_rows, with_lse, rider
        )
        results[d] = [send(part, ctx_count - d) for part in answer]

    pieces = [packed[1], arrived[1], results[last][0]][: reach + 1]
    pieces = [(piece, q_rows) for piece in pieces]
    for _ in range(len(pieces), reach + 1):
        array, first = pieces[-1]
        rows = 2 * kv_used * tok_rows
        pieces.append((send(array[first : first + rows], 1), 0))
    self_out = attend_self(where, doc_lengths, q_self, pieces[::-1], kv_used)
    gate_cols = jnp.repeat(jnp.tanh(cross_gate), HEAD_DIM)[None, :]
    partials = [results[d][0] for d in range(ctx_count)]
    if one_owner:
        return mix(where, pair_tiles, tile_slot, gate_cols, self_out, partials, tiles_dev)
    partials = [partial[:q_rows] for partial in partials]
    sums = [results[d][1] for d in range(ctx_count)]
    return mix_owners(where, pair_tiles, tile_slot, gate_cols, self_out, partials, sums, tiles_dev)


def solution(mesh):
    in_specs = (
        P(("groups", "ctx"), ("head", "rep")),
        P(("groups", "ctx"), ("head", "rep")),
        P(None, ("groups", "ctx"), "head"),
        P(None, ("groups", "ctx"), None, "head"),
        P(("head", "rep")),
        P("groups"),
        P(("groups", "ctx"), None),
        P("groups"),
    )
    out_specs = P(("groups", "ctx"), ("head", "rep"))
    return jax.shard_map(attend, mesh=mesh, in_specs=in_specs, out_specs=out_specs, check_vma=False)
```

```python
import functools
import math

import jax
import jax.numpy as jnp
from jax import lax
from jax.experimental import pallas as pl
from jax.experimental.pallas import tpu as pltpu
from jax.sharding import PartitionSpec as P


HEAD_DIM = 128
Q_HEADS = 64
KV_HEADS = 8
BLOCK = 32
PAIRS = 4

NEG_FILL = -1e30
META_ROWS = 8
KEY_CHUNK = 256
LAG = 2
MOST_TOTAL = 2.0**100
LOG2E = math.log2(math.e)
EXP2_SCALE = HEAD_DIM ** (-0.5) * LOG2E

SMEM = pl.BlockSpec(memory_space=pltpu.SMEM)
VMEM = pl.BlockSpec(memory_space=pltpu.VMEM)
HBM = pl.BlockSpec(memory_space=pltpu.HBM)
PARAMS = pltpu.CompilerParams(vmem_limit_bytes=24 << 20)


def in_vmem(array):
    return pltpu.with_memory_space_constraint(array, pltpu.VMEM)


def in_hbm(array):
    return pltpu.with_memory_space_constraint(array, pltpu.HBM)


def owner_slots(pairs_ref, slots_ref):
    blocks, pairs = pairs_ref.shape
    return [[slots_ref[pairs_ref[b, p]] for p in range(pairs)] for b in range(blocks)]


def block_for(stored, owner, tiles_dev):
    block = jnp.int32(0)
    counts = [jnp.int32(0)] * tiles_dev
    for b, row in enumerate(stored):
        for slot in row:
            tile = slot - owner * tiles_dev
            block = jnp.where((tile >= 0) & (tile < tiles_dev), jnp.int32(b), block)
            counts = [n + (tile == i).astype(jnp.int32) for i, n in enumerate(counts)]
    return block, counts


def pack_body(
    pairs_hbm, slots_hbm, q_hbm, kv_hbm, *refs, tiles_dev, kv_used, kv_first
):
    out_refs = refs[:-5]
    q_ref, pairs_ref, slots_ref, kv_sem, sem = refs[-5:]
    ctx_count = len(out_refs)
    heads = q_ref.shape[1] // HEAD_DIM
    tok_rows = kv_hbm.shape[1]
    kv_at = heads * BLOCK
    tables = [
        pltpu.make_async_copy(pairs_hbm, pairs_ref, sem.at[0]),
        pltpu.make_async_copy(slots_hbm, slots_ref, sem.at[1]),
    ]
    queries = pltpu.make_async_copy(q_hbm, q_ref, sem.at[2])
    copies = []
    for w in range(2):
        for k in range(kv_used):
            cols = pl.ds(pl.multiple_of((kv_first() + k) * HEAD_DIM, HEAD_DIM), HEAD_DIM)
            part = w * kv_used + k
            rows = pl.ds(kv_at + part * tok_rows, tok_rows)
            copies.append(
                pltpu.make_async_copy(kv_hbm.at[w, :, cols], out_refs[1].at[rows, :], kv_sem.at[part])
            )
    for copy in tables + [queries] + copies:
        copy.start()
    for copy in tables:
        copy.wait()
    stored = owner_slots(pairs_ref, slots_ref)
    here = lax.axis_index("ctx")
    lanes = lax.broadcasted_iota(jnp.int32, (META_ROWS, HEAD_DIM), 1)
    blocks = []
    for distance, out_ref in enumerate(out_refs):
        owner = lax.rem(here + distance, ctx_count)
        block, counts = block_for(stored, owner, tiles_dev)
        blocks.append(block)
        meta = jnp.zeros((META_ROWS, HEAD_DIM), jnp.float32)
        for i, n in enumerate(counts):
            meta = jnp.where(lanes % tiles_dev == i, n.astype(jnp.float32), meta)
        out_ref[out_ref.shape[0] - META_ROWS :, :] = meta.astype(jnp.bfloat16)
    queries.wait()
    for block, out_ref in zip(blocks, out_refs):
        rows = pl.ds(pl.multiple_of(block * BLOCK, BLOCK), BLOCK)
        for h in range(heads):
            out_ref[h * BLOCK : (h + 1) * BLOCK, :] = q_ref[rows, h * HEAD_DIM : (h + 1) * HEAD_DIM]
    for copy in copies:
        copy.wait()


def pack_queries(pair_tiles, tile_slot, q_cross, kv_self, ctx_count, tiles_dev, kv_used, kv_first):
    rows = q_cross.shape[1] // HEAD_DIM * BLOCK + META_ROWS
    kv_rows = 2 * kv_used * kv_self.shape[1]
    return pl.pallas_call(
        functools.partial(pack_body, tiles_dev=tiles_dev, kv_used=kv_used, kv_first=kv_first),
        out_shape=[
            pltpu.VMEM((rows + (kv_rows if d == 1 else 0), HEAD_DIM), jnp.bfloat16)
            for d in range(ctx_count)
        ],
        in_specs=[HBM] * 4,
        out_specs=[VMEM] * ctx_count,
        scratch_shapes=[
            pltpu.VMEM(q_cross.shape, q_cross.dtype),
            pltpu.SMEM(pair_tiles.shape, jnp.int32),
            pltpu.SMEM(tile_slot.shape, jnp.int32),
            pltpu.SemaphoreType.DMA((2 * kv_used,)),
            pltpu.SemaphoreType.DMA((3,)),
        ],
        compiler_params=PARAMS,
        name="pack_queries",
    )(in_hbm(pair_tiles), in_hbm(tile_slot), in_hbm(q_cross), in_hbm(kv_self))


def count_bias(meta):
    count = meta[0:1, :].astype(jnp.float32)
    return jnp.where(count > 0, jnp.log(jnp.maximum(count, 1.0)) * LOG2E, NEG_FILL)


def finish_head(blended, total, best):
    live = total > 0
    total = jnp.where(live, total, 1.0)
    out = (blended / total).astype(jnp.bfloat16)
    lse = jnp.where(live, best * (1.0 / LOG2E) + jnp.log(total), NEG_FILL)
    return out, jnp.broadcast_to(lse, (lse.shape[0], HEAD_DIM))


def attend_head(q, meta, keys, values, key_count, wait_values):
    rows = q.shape[0]
    padded = keys.shape[0]
    lanes = HEAD_DIM
    bias = count_bias(meta)

    def score(at, size):
        return lax.dot_general(
            q, keys[at : at + size, :], (((1,), (1,)), ((), ())), preferred_element_type=jnp.float32
        )

    first = score(0, KEY_CHUNK)
    best = first[:, :lanes]
    for col in range(lanes, KEY_CHUNK, lanes):
        best = jnp.maximum(best, first[:, col : col + lanes])
    best = jnp.max(best * EXP2_SCALE + bias, axis=1, keepdims=True)
    shift = jnp.where(best > 0.5 * NEG_FILL, bias - best, NEG_FILL)
    totals = jnp.zeros((rows, lanes), jnp.float32)
    total = jnp.zeros((rows, 1), jnp.float32)
    blended = jnp.zeros((rows, HEAD_DIM), jnp.float32)
    waiting = []
    wait_values()
    for at in list(range(0, padded, KEY_CHUNK)) + [None] * LAG:
        if at is not None:
            size = min(KEY_CHUNK, padded - at)
            scores = score(at, size)
            pieces = []
            for col in range(0, size, lanes):
                width = min(lanes, size - col)
                weights = jnp.exp2(scores[:, col : col + width] * EXP2_SCALE + shift[:, :width])
                valid = key_count - at - col
                if width > valid:
                    held = lax.broadcasted_iota(jnp.int32, weights.shape, 1) < valid
                    weights = jnp.where(held, weights, 0.0)
                if width == lanes:
                    totals = totals + weights
                else:
                    total = total + jnp.sum(weights, axis=1, keepdims=True)
                pieces.append(weights.astype(jnp.bfloat16))
            weights = jnp.concatenate(pieces, axis=1) if len(pieces) > 1 else pieces[0]
            waiting.append((weights, at))
        if len(waiting) > LAG or at is None:
            weights, start = waiting.pop(0)
            blended = blended + jnp.dot(
                weights,
                values[start : start + weights.shape[1], :],
                preferred_element_type=jnp.float32,
            )
    total = total + jnp.sum(totals, axis=1, keepdims=True)
    return *finish_head(blended, total, best), total


def attend_head_exact(q, meta, keys, values, key_count, scores_sc):
    rows = q.shape[0]
    padded = keys.shape[0]
    lanes = HEAD_DIM
    bias = count_bias(meta)
    best = None
    for at in range(0, padded, KEY_CHUNK):
        size = min(KEY_CHUNK, padded - at)
        scores = lax.dot_general(
            q, keys[at : at + size, :], (((1,), (1,)), ((), ())), preferred_element_type=jnp.float32
        )
        for col in range(0, size, lanes):
            width = min(lanes, size - col)
            piece = scores[:, col : col + width]
            valid = key_count - at - col
            if width > valid:
                piece = jnp.where(lax.broadcasted_iota(jnp.int32, piece.shape, 1) < valid, piece, NEG_FILL)
            scores_sc[:, at + col : at + col + width] = piece
            if width == lanes:
                best = piece if best is None else jnp.maximum(best, piece)
            else:
                tail = piece
    best = jnp.max(best * EXP2_SCALE + bias, axis=1, keepdims=True)
    tail_width = padded % lanes
    if tail_width:
        tail = jnp.max(tail * EXP2_SCALE + bias[:, :tail_width], axis=1, keepdims=True)
        best = jnp.maximum(best, tail)
    shift = jnp.where(best > 0.5 * NEG_FILL, bias - best, NEG_FILL)
    totals = jnp.zeros((rows, lanes), jnp.float32)
    total = jnp.zeros((rows, 1), jnp.float32)
    blended = jnp.zeros((rows, HEAD_DIM), jnp.float32)
    for at in range(0, padded, KEY_CHUNK):
        size = min(KEY_CHUNK, padded - at)
        pieces = []
        for col in range(0, size, lanes):
            width = min(lanes, size - col)
            piece = scores_sc[:, at + col : at + col + width]
            weights = jnp.exp2(piece * EXP2_SCALE + shift[:, :width])
            if width == lanes:
                totals = totals + weights
            else:
                total = total + jnp.sum(weights, axis=1, keepdims=True)
            pieces.append(weights.astype(jnp.bfloat16))
        weights = jnp.concatenate(pieces, axis=1) if len(pieces) > 1 else pieces[0]
        blended = blended + jnp.dot(
            weights, values[at : at + size, :], preferred_element_type=jnp.float32
        )
    total = total + jnp.sum(totals, axis=1, keepdims=True)
    return finish_head(blended, total, best)


def attend_block(q_ref, keys_ref, values_ref, out_ref, lse_ref, scores_sc, key_count, wait):
    kv_used = keys_ref.shape[0]
    rows = scores_sc.shape[0]
    meta = q_ref[q_ref.shape[0] - META_ROWS :, :]

    def place(k):
        return slice(k * rows, (k + 1) * rows)

    def store(k, out, lse):
        out_ref[place(k), :] = out
        if lse_ref is not None:
            lse_ref[place(k), :] = lse

    highest = jnp.zeros((rows, 1), jnp.float32)
    for k in range(kv_used):
        wait_values = wait(k)
        keys, values = keys_ref.at[k], values_ref.at[k]
        out, lse, total = attend_head(q_ref[place(k), :], meta, keys, values, key_count, wait_values)
        store(k, out, lse)
        highest = jnp.maximum(highest, total)

    @pl.when(jnp.logical_not(jnp.max(highest) <= MOST_TOTAL))
    def _():
        for k in range(kv_used):
            keys, values = keys_ref.at[k], values_ref.at[k]
            store(
                k,
                *attend_head_exact(q_ref[place(k), :], meta, keys, values, key_count, scores_sc),
            )


def no_wait(k):
    return lambda: None


def own_body(where_ref, q_ref, image_hbm, *refs, with_lse):
    out_ref = refs[0]
    lse_ref = refs[1] if with_lse else None
    keys_ref, values_ref, scores_sc, sem = refs[-4:]
    _, tile_len, tiles_dev, width = image_hbm.shape
    key_count = tile_len * tiles_dev
    kv_used, padded = keys_ref.shape[:2]
    image = image_hbm.reshape(2, key_count, width)

    def copies(k):
        cols = pl.ds(pl.multiple_of((where_ref[1] + k) * HEAD_DIM, HEAD_DIM), HEAD_DIM)
        held = pl.ds(0, key_count)
        return [
            pltpu.make_async_copy(image.at[w, :, cols], ref.at[k, held], sem.at[w, k])
            for w, ref in enumerate((keys_ref, values_ref))
        ]

    for copy in copies(0):
        copy.start()
    if padded > key_count:
        pad = jnp.zeros((padded - key_count, HEAD_DIM), jnp.bfloat16)
        for k in range(kv_used):
            keys_ref[k, key_count:, :] = pad
            values_ref[k, key_count:, :] = pad

    def wait(k):
        keys, values = copies(k)
        keys.wait()
        if k == 0:
            for later in range(1, kv_used):
                for copy in copies(later):
                    copy.start()
        return values.wait

    attend_block(
        q_ref, keys_ref, values_ref, out_ref, lse_ref, scores_sc, key_count, wait
    )


def attend_own(where, packed, image_kv, kv_used, q_rows, with_lse):
    _, tile_len, tiles_dev, _ = image_kv.shape
    padded = -(-tile_len * tiles_dev // 16) * 16
    held = pltpu.VMEM((kv_used, padded, HEAD_DIM), jnp.bfloat16)
    out_shape = [pltpu.VMEM((q_rows, HEAD_DIM), jnp.bfloat16)]
    if with_lse:
        out_shape.append(pltpu.VMEM((q_rows, HEAD_DIM), jnp.float32))
    out_shape += [held, held]
    results = pl.pallas_call(
        functools.partial(own_body, with_lse=with_lse),
        out_shape=out_shape,
        in_specs=[SMEM, VMEM, HBM],
        out_specs=[VMEM] * len(out_shape),
        scratch_shapes=[
            pltpu.VMEM((q_rows // kv_used, padded), jnp.float32),
            pltpu.SemaphoreType.DMA((2, kv_used)),
        ],
        compiler_params=PARAMS,
        name="attend_own",
    )(where, in_vmem(packed), in_hbm(image_kv))
    return results[:-2], [in_vmem(part) for part in results[-2:]]


def arrived_body(q_ref, keys_ref, values_ref, out_ref, *refs, with_lse, key_count):
    lse_ref = refs[0] if with_lse else None
    attend_block(
        q_ref, keys_ref, values_ref, out_ref, lse_ref, refs[-1], key_count, no_wait
    )


def attend_arrived(packed, held, key_count, q_rows, with_lse):
    kv_used, padded, _ = held[0].shape
    out_shape = [pltpu.VMEM((q_rows, HEAD_DIM), jnp.bfloat16)]
    if with_lse:
        out_shape.append(pltpu.VMEM((q_rows, HEAD_DIM), jnp.float32))
    return pl.pallas_call(
        functools.partial(arrived_body, with_lse=with_lse, key_count=key_count),
        out_shape=out_shape,
        in_specs=[VMEM] * 3,
        out_specs=[VMEM] * len(out_shape),
        scratch_shapes=[pltpu.VMEM((q_rows // kv_used, padded), jnp.float32)],
        compiler_params=PARAMS,
        name="attend_arrived",
    )(in_vmem(packed), *held)


def join_body(partial_ref, message_ref, out_ref):
    q_rows = partial_ref.shape[0]
    out_ref[:q_rows, :] = partial_ref[...]
    out_ref[q_rows:, :] = message_ref[q_rows : out_ref.shape[0], :]


def join_keys(partial, message):
    return pl.pallas_call(
        join_body,
        out_shape=pltpu.VMEM((message.shape[0] - META_ROWS, HEAD_DIM), jnp.bfloat16),
        in_specs=[VMEM] * 2,
        out_specs=VMEM,
        compiler_params=PARAMS,
        name="join_keys",
    )(in_vmem(partial), in_vmem(message))


def self_body(where_ref, docs_ref, q_ref, *refs, starts, kv_used):
    kv_refs, out_ref, bias_sc = refs[:-2], refs[-2], refs[-1]
    tok_rows, q_width = q_ref.shape
    per_kv = q_width // HEAD_DIM // kv_used
    shape = bias_sc.shape
    row_start = where_ref[0] * tok_rows
    query_pos = row_start + lax.broadcasted_iota(jnp.int32, (tok_rows, 1), 0)
    key_pos = row_start + tok_rows - shape[1] + lax.broadcasted_iota(jnp.int32, shape, 1)
    doc_start = jnp.zeros((tok_rows, 1), jnp.int32)
    doc_end = jnp.int32(0)
    for j in range(docs_ref.shape[0]):
        doc_end = doc_end + docs_ref[j]
        doc_start = jnp.where(query_pos >= doc_end, doc_end, doc_start)
    bias_sc[...] = jnp.where((key_pos <= query_pos) & (key_pos >= doc_start), 0.0, NEG_FILL)
    for k in range(kv_used):
        keys, values = [
            jnp.concatenate(
                [
                    ref[at + (w * kv_used + k) * tok_rows : at + (w * kv_used + k + 1) * tok_rows, :]
                    for ref, at in zip(kv_refs, starts)
                ],
                axis=0,
            )
            for w in range(2)
        ]
        heads = range(k * per_kv, (k + 1) * per_kv)
        q = jnp.concatenate([q_ref[:, h * HEAD_DIM : (h + 1) * HEAD_DIM] for h in heads], axis=0)
        scores = lax.dot_general(
            q, keys, (((1,), (1,)), ((), ())), preferred_element_type=jnp.float32
        )
        scores = scores * EXP2_SCALE + jnp.concatenate([bias_sc[...]] * per_kv, axis=0)
        row_best = jnp.max(scores, axis=1, keepdims=True)
        weights = jnp.exp2(scores - row_best)
        row_total = jnp.sum(weights, axis=1, keepdims=True)
        blended = jnp.dot(weights.astype(jnp.bfloat16), values, preferred_element_type=jnp.float32)
        blended = blended / row_total
        for i, h in enumerate(heads):
            out_ref[:, h * HEAD_DIM : (h + 1) * HEAD_DIM] = blended[i * tok_rows : (i + 1) * tok_rows]


def attend_self(where, doc_lengths, q_self, pieces, kv_used):
    tok_rows, q_width = q_self.shape
    return pl.pallas_call(
        functools.partial(self_body, starts=[at for _, at in pieces], kv_used=kv_used),
        out_shape=pltpu.VMEM((tok_rows, q_width), jnp.float32),
        in_specs=[SMEM, SMEM] + [VMEM] * (1 + len(pieces)),
        out_specs=VMEM,
        scratch_shapes=[pltpu.VMEM((tok_rows, len(pieces) * tok_rows), jnp.float32)],
        compiler_params=PARAMS,
        name="attend_self",
    )(where, doc_lengths, in_vmem(q_self), *[in_vmem(array) for array, _ in pieces])


def mix_body(pairs_ref, slots_ref, gate_ref, self_ref, *refs, tiles_dev):
    partial_refs, (out_hbm, out_ref, sem) = refs[:-3], refs[-3:]
    stored = owner_slots(pairs_ref, slots_ref)
    here = lax.axis_index("ctx")
    copies = []
    for distance, partial_ref in enumerate(partial_refs):
        owner = lax.rem(here + distance, len(partial_refs))
        block, _ = block_for(stored, owner, tiles_dev)
        rows = pl.ds(pl.multiple_of(block * BLOCK, BLOCK), BLOCK)
        for h in range(self_ref.shape[1] // HEAD_DIM):
            cols = slice(h * HEAD_DIM, (h + 1) * HEAD_DIM)
            cross = partial_ref[h * BLOCK : (h + 1) * BLOCK, :].astype(jnp.float32)
            mixed = self_ref[rows, cols] + gate_ref[:, cols] * cross
            out_ref[rows, cols] = mixed.astype(jnp.bfloat16)
        copy = pltpu.make_async_copy(out_ref.at[rows, :], out_hbm.at[rows, :], sem.at[distance])
        copy.start()
        copies.append(copy)
    for copy in copies:
        copy.wait()


def mix(pair_tiles, tile_slot, gate_cols, self_out, partials, tiles_dev):
    out = jax.ShapeDtypeStruct(self_out.shape, jnp.bfloat16)
    return pl.pallas_call(
        functools.partial(mix_body, tiles_dev=tiles_dev),
        out_shape=out,
        in_specs=[SMEM] * 2 + [VMEM] * (2 + len(partials)),
        out_specs=HBM,
        scratch_shapes=[
            pltpu.VMEM(out.shape, out.dtype),
            pltpu.SemaphoreType.DMA((len(partials),)),
        ],
        compiler_params=PARAMS,
        name="mix",
    )(
        pair_tiles,
        tile_slot,
        in_vmem(gate_cols),
        in_vmem(self_out),
        *[in_vmem(partial) for partial in partials],
    )


def mix_owners(where, pair_tiles, tile_slot, gate_cols, self_out, partials, sums, tiles_dev):
    block_count = pair_tiles.shape[0]
    tok_rows, q_width = self_out.shape
    heads = q_width // HEAD_DIM
    ctx_count = len(partials)
    owners = jnp.take(tile_slot, pair_tiles.reshape(-1), axis=0).reshape(block_count, -1) // tiles_dev
    partners = (where[0] + jnp.arange(ctx_count, dtype=jnp.int32)) % ctx_count
    live = jnp.any(owners[:, :, None] == partners[None, None, :], axis=1)[:, :, None, None]
    lse = jnp.stack(sums)[None]
    top = jnp.max(jnp.where(live, lse, NEG_FILL), axis=1, keepdims=True)
    factors = jnp.where(live, jnp.exp(lse - top), 0.0)
    pieces = jnp.stack(partials).astype(jnp.float32)[None]
    cross = jnp.sum(factors * pieces, axis=1) / jnp.sum(factors, axis=1)
    cross = jnp.transpose(cross.reshape(block_count, heads, BLOCK, HEAD_DIM), (0, 2, 1, 3))
    return (self_out + gate_cols * cross.reshape(tok_rows, q_width)).astype(jnp.bfloat16)


def partner_order(ctx_count):
    return list(range(ctx_count - 1, 0, -1))


def attend(q_self, q_cross, kv_self, image_kv, cross_gate, doc_lengths, pair_tiles, tile_slot):
    tok_rows, q_width = q_self.shape
    local_heads = q_width // HEAD_DIM
    q_rows = local_heads * BLOCK
    grouping = Q_HEADS // KV_HEADS
    per_kv = min(local_heads, grouping)
    kv_used = local_heads // per_kv
    ctx_count = lax.axis_size("ctx")
    tiles_dev, tile_len = image_kv.shape[1:3]
    request_count = pair_tiles.shape[0] * PAIRS
    capacity = max(2, -(-request_count // ctx_count))
    one_owner = ctx_count * capacity == request_count and capacity == PAIRS
    with_lse = not one_owner
    reach = min(ctx_count - 1, -(-(ctx_count * tok_rows // 2 - 1) // tok_rows))

    here = lax.axis_index("ctx").astype(jnp.int32)

    def kv_first():
        return lax.axis_index("rep") * local_heads // grouping

    where = jnp.stack([here, kv_first().astype(jnp.int32)])
    image_kv = jnp.transpose(image_kv, (0, 2, 1, 3))

    def send(array, distance):
        pairs = [(i, (i + distance) % ctx_count) for i in range(ctx_count)]
        return lax.ppermute(array, "ctx", pairs)

    packed = pack_queries(
        pair_tiles, tile_slot, q_cross, kv_self, ctx_count, tiles_dev, kv_used, kv_first
    )
    last = ctx_count - 1
    order = partner_order(ctx_count)
    arrived = {d: send(packed[d], d) for d in order[-1:] + order[:-1]}
    results = {}
    results[0], held = attend_own(where, packed[0], image_kv, kv_used, q_rows, with_lse)
    for d in order:
        answer = attend_arrived(arrived[d], held, tile_len * tiles_dev, q_rows, with_lse)
        if d == last:
            answer = [join_keys(answer[0], arrived[1]), *answer[1:]]
        results[d] = [send(part, ctx_count - d) for part in answer]

    pieces = [packed[1], arrived[1], results[last][0]][: reach + 1]
    pieces = [(piece, q_rows) for piece in pieces]
    for _ in range(len(pieces), reach + 1):
        array, first = pieces[-1]
        rows = 2 * kv_used * tok_rows
        pieces.append((send(array[first : first + rows], 1), 0))
    self_out = attend_self(where, doc_lengths, q_self, pieces[::-1], kv_used)
    gate_cols = jnp.repeat(jnp.tanh(cross_gate), HEAD_DIM)[None, :]
    partials = [results[d][0] for d in range(ctx_count)]
    if one_owner:
        return mix(pair_tiles, tile_slot, gate_cols, self_out, partials, tiles_dev)
    partials = [partial[:q_rows] for partial in partials]
    sums = [results[d][1] for d in range(ctx_count)]
    return mix_owners(where, pair_tiles, tile_slot, gate_cols, self_out, partials, sums, tiles_dev)


def solution(mesh):
    in_specs = (
        P(("groups", "ctx"), ("head", "rep")),
        P(("groups", "ctx"), ("head", "rep")),
        P(None, ("groups", "ctx"), "head"),
        P(None, ("groups", "ctx"), None, "head"),
        P(("head", "rep")),
        P("groups"),
        P(("groups", "ctx"), None),
        P("groups"),
    )
    out_specs = P(("groups", "ctx"), ("head", "rep"))
    return jax.shard_map(attend, mesh=mesh, in_specs=in_specs, out_specs=out_specs, check_vma=False)
```

```python
import functools
import math

import jax
import jax.numpy as jnp
from jax import lax
from jax.experimental import pallas as pl
from jax.experimental.pallas import tpu as pltpu
from jax.sharding import PartitionSpec as P


HEAD_DIM = 128
Q_HEADS = 64
KV_HEADS = 8
BLOCK = 32
PAIRS = 4

NEG_FILL = -1e30
META_ROWS = 8
KEY_CHUNK = 256
LAG = 2
MOST_TOTAL = 2.0**100
LOG2E = math.log2(math.e)
EXP2_SCALE = HEAD_DIM ** (-0.5) * LOG2E

SMEM = pl.BlockSpec(memory_space=pltpu.SMEM)
VMEM = pl.BlockSpec(memory_space=pltpu.VMEM)
HBM = pl.BlockSpec(memory_space=pltpu.HBM)
PARAMS = pltpu.CompilerParams(vmem_limit_bytes=24 << 20)


def in_vmem(array):
    return pltpu.with_memory_space_constraint(array, pltpu.VMEM)


def in_hbm(array):
    return pltpu.with_memory_space_constraint(array, pltpu.HBM)


def owner_slots(pairs_ref, slots_ref):
    blocks, pairs = pairs_ref.shape
    return [[slots_ref[pairs_ref[b, p]] for p in range(pairs)] for b in range(blocks)]


def block_for(stored, owner, tiles_dev):
    block = jnp.int32(0)
    counts = [jnp.int32(0)] * tiles_dev
    for b, row in enumerate(stored):
        for slot in row:
            tile = slot - owner * tiles_dev
            block = jnp.where((tile >= 0) & (tile < tiles_dev), jnp.int32(b), block)
            counts = [n + (tile == i).astype(jnp.int32) for i, n in enumerate(counts)]
    return block, counts


def pack_body(
    pairs_hbm, slots_hbm, q_hbm, kv_hbm, *refs, tiles_dev, kv_used, kv_first
):
    out_refs = refs[:-5]
    q_ref, pairs_ref, slots_ref, kv_sem, sem = refs[-5:]
    ctx_count = len(out_refs)
    heads = q_ref.shape[1] // HEAD_DIM
    tok_rows = kv_hbm.shape[1]
    kv_at = heads * BLOCK
    tables = [
        pltpu.make_async_copy(pairs_hbm, pairs_ref, sem.at[0]),
        pltpu.make_async_copy(slots_hbm, slots_ref, sem.at[1]),
    ]
    queries = pltpu.make_async_copy(q_hbm, q_ref, sem.at[2])
    copies = []
    for w in range(2):
        for k in range(kv_used):
            cols = pl.ds(pl.multiple_of((kv_first() + k) * HEAD_DIM, HEAD_DIM), HEAD_DIM)
            part = w * kv_used + k
            rows = pl.ds(kv_at + part * tok_rows, tok_rows)
            copies.append(
                pltpu.make_async_copy(kv_hbm.at[w, :, cols], out_refs[1].at[rows, :], kv_sem.at[part])
            )
    for copy in tables + [queries] + copies:
        copy.start()
    for copy in tables:
        copy.wait()
    stored = owner_slots(pairs_ref, slots_ref)
    here = lax.axis_index("ctx")
    lanes = lax.broadcasted_iota(jnp.int32, (META_ROWS, HEAD_DIM), 1)
    blocks = []
    for distance, out_ref in enumerate(out_refs):
        owner = lax.rem(here + distance, ctx_count)
        block, counts = block_for(stored, owner, tiles_dev)
        blocks.append(block)
        meta = jnp.zeros((META_ROWS, HEAD_DIM), jnp.float32)
        for i, n in enumerate(counts):
            meta = jnp.where(lanes % tiles_dev == i, n.astype(jnp.float32), meta)
        out_ref[out_ref.shape[0] - META_ROWS :, :] = meta.astype(jnp.bfloat16)
    queries.wait()
    for block, out_ref in zip(blocks, out_refs):
        rows = pl.ds(pl.multiple_of(block * BLOCK, BLOCK), BLOCK)
        for h in range(heads):
            out_ref[h * BLOCK : (h + 1) * BLOCK, :] = q_ref[rows, h * HEAD_DIM : (h + 1) * HEAD_DIM]
    for copy in copies:
        copy.wait()


def pack_queries(pair_tiles, tile_slot, q_cross, kv_self, ctx_count, tiles_dev, kv_used, kv_first):
    rows = q_cross.shape[1] // HEAD_DIM * BLOCK + META_ROWS
    kv_rows = 2 * kv_used * kv_self.shape[1]
    return pl.pallas_call(
        functools.partial(pack_body, tiles_dev=tiles_dev, kv_used=kv_used, kv_first=kv_first),
        out_shape=[
            pltpu.VMEM((rows + (kv_rows if d == 1 else 0), HEAD_DIM), jnp.bfloat16)
            for d in range(ctx_count)
        ],
        in_specs=[HBM] * 4,
        out_specs=[VMEM] * ctx_count,
        scratch_shapes=[
            pltpu.VMEM(q_cross.shape, q_cross.dtype),
            pltpu.SMEM(pair_tiles.shape, jnp.int32),
            pltpu.SMEM(tile_slot.shape, jnp.int32),
            pltpu.SemaphoreType.DMA((2 * kv_used,)),
            pltpu.SemaphoreType.DMA((3,)),
        ],
        compiler_params=PARAMS,
        name="pack_queries",
    )(in_hbm(pair_tiles), in_hbm(tile_slot), in_hbm(q_cross), in_hbm(kv_self))


def count_bias(meta):
    count = meta[0:1, :].astype(jnp.float32)
    return jnp.where(count > 0, jnp.log(jnp.maximum(count, 1.0)) * LOG2E, NEG_FILL)


def finish_head(blended, total, best):
    live = total > 0
    total = jnp.where(live, total, 1.0)
    out = (blended / total).astype(jnp.bfloat16)
    lse = jnp.where(live, best * (1.0 / LOG2E) + jnp.log(total), NEG_FILL)
    return out, jnp.broadcast_to(lse, (lse.shape[0], HEAD_DIM))


def attend_head(q, meta, keys, values, key_count, wait_values):
    rows = q.shape[0]
    padded = keys.shape[0]
    lanes = HEAD_DIM
    bias = count_bias(meta)

    def score(at, size):
        return lax.dot_general(
            q, keys[at : at + size, :], (((1,), (1,)), ((), ())), preferred_element_type=jnp.float32
        )

    first = score(0, KEY_CHUNK)
    best = first[:, :lanes]
    for col in range(lanes, KEY_CHUNK, lanes):
        best = jnp.maximum(best, first[:, col : col + lanes])
    best = jnp.max(best * EXP2_SCALE + bias, axis=1, keepdims=True)
    shift = jnp.where(best > 0.5 * NEG_FILL, bias - best, NEG_FILL)
    totals = jnp.zeros((rows, lanes), jnp.float32)
    total = jnp.zeros((rows, 1), jnp.float32)
    blended = jnp.zeros((rows, HEAD_DIM), jnp.float32)
    waiting = []
    wait_values()
    for at in list(range(0, padded, KEY_CHUNK)) + [None] * LAG:
        if at is not None:
            size = min(KEY_CHUNK, padded - at)
            scores = score(at, size)
            pieces = []
            for col in range(0, size, lanes):
                width = min(lanes, size - col)
                weights = jnp.exp2(scores[:, col : col + width] * EXP2_SCALE + shift[:, :width])
                valid = key_count - at - col
                if width > valid:
                    held = lax.broadcasted_iota(jnp.int32, weights.shape, 1) < valid
                    weights = jnp.where(held, weights, 0.0)
                if width == lanes:
                    totals = totals + weights
                else:
                    total = total + jnp.sum(weights, axis=1, keepdims=True)
                pieces.append(weights.astype(jnp.bfloat16))
            weights = jnp.concatenate(pieces, axis=1) if len(pieces) > 1 else pieces[0]
            waiting.append((weights, at))
        if len(waiting) > LAG or at is None:
            weights, start = waiting.pop(0)
            blended = blended + jnp.dot(
                weights,
                values[start : start + weights.shape[1], :],
                preferred_element_type=jnp.float32,
            )
    total = total + jnp.sum(totals, axis=1, keepdims=True)
    return *finish_head(blended, total, best), total


def attend_head_exact(q, meta, keys, values, key_count, scores_sc):
    rows = q.shape[0]
    padded = keys.shape[0]
    lanes = HEAD_DIM
    bias = count_bias(meta)
    best = None
    for at in range(0, padded, KEY_CHUNK):
        size = min(KEY_CHUNK, padded - at)
        scores = lax.dot_general(
            q, keys[at : at + size, :], (((1,), (1,)), ((), ())), preferred_element_type=jnp.float32
        )
        for col in range(0, size, lanes):
            width = min(lanes, size - col)
            piece = scores[:, col : col + width]
            valid = key_count - at - col
            if width > valid:
                piece = jnp.where(lax.broadcasted_iota(jnp.int32, piece.shape, 1) < valid, piece, NEG_FILL)
            scores_sc[:, at + col : at + col + width] = piece
            if width == lanes:
                best = piece if best is None else jnp.maximum(best, piece)
            else:
                tail = piece
    best = jnp.max(best * EXP2_SCALE + bias, axis=1, keepdims=True)
    tail_width = padded % lanes
    if tail_width:
        tail = jnp.max(tail * EXP2_SCALE + bias[:, :tail_width], axis=1, keepdims=True)
        best = jnp.maximum(best, tail)
    shift = jnp.where(best > 0.5 * NEG_FILL, bias - best, NEG_FILL)
    totals = jnp.zeros((rows, lanes), jnp.float32)
    total = jnp.zeros((rows, 1), jnp.float32)
    blended = jnp.zeros((rows, HEAD_DIM), jnp.float32)
    for at in range(0, padded, KEY_CHUNK):
        size = min(KEY_CHUNK, padded - at)
        pieces = []
        for col in range(0, size, lanes):
            width = min(lanes, size - col)
            piece = scores_sc[:, at + col : at + col + width]
            weights = jnp.exp2(piece * EXP2_SCALE + shift[:, :width])
            if width == lanes:
                totals = totals + weights
            else:
                total = total + jnp.sum(weights, axis=1, keepdims=True)
            pieces.append(weights.astype(jnp.bfloat16))
        weights = jnp.concatenate(pieces, axis=1) if len(pieces) > 1 else pieces[0]
        blended = blended + jnp.dot(
            weights, values[at : at + size, :], preferred_element_type=jnp.float32
        )
    total = total + jnp.sum(totals, axis=1, keepdims=True)
    return finish_head(blended, total, best)


def attend_block(q_ref, keys_ref, values_ref, out_ref, lse_ref, scores_sc, key_count, wait):
    kv_used = keys_ref.shape[0]
    rows = scores_sc.shape[0]
    meta = q_ref[q_ref.shape[0] - META_ROWS :, :]

    def place(k):
        return slice(k * rows, (k + 1) * rows)

    def store(k, out, lse):
        out_ref[place(k), :] = out
        if lse_ref is not None:
            lse_ref[place(k), :] = lse

    highest = jnp.zeros((rows, 1), jnp.float32)
    for k in range(kv_used):
        wait_values = wait(k)
        keys, values = keys_ref.at[k], values_ref.at[k]
        out, lse, total = attend_head(q_ref[place(k), :], meta, keys, values, key_count, wait_values)
        store(k, out, lse)
        highest = jnp.maximum(highest, total)

    @pl.when(jnp.logical_not(jnp.max(highest) <= MOST_TOTAL))
    def _():
        for k in range(kv_used):
            keys, values = keys_ref.at[k], values_ref.at[k]
            store(
                k,
                *attend_head_exact(q_ref[place(k), :], meta, keys, values, key_count, scores_sc),
            )


def no_wait(k):
    return lambda: None


def own_body(where_ref, q_ref, image_hbm, *refs, with_lse):
    out_ref = refs[0]
    lse_ref = refs[1] if with_lse else None
    keys_ref, values_ref, scores_sc, sem = refs[-4:]
    _, tile_len, tiles_dev, width = image_hbm.shape
    key_count = tile_len * tiles_dev
    kv_used, padded = keys_ref.shape[:2]
    image = image_hbm.reshape(2, key_count, width)

    def copies(k):
        cols = pl.ds(pl.multiple_of((where_ref[1] + k) * HEAD_DIM, HEAD_DIM), HEAD_DIM)
        held = pl.ds(0, key_count)
        return [
            pltpu.make_async_copy(image.at[w, :, cols], ref.at[k, held], sem.at[w, k])
            for w, ref in enumerate((keys_ref, values_ref))
        ]

    for copy in copies(0):
        copy.start()
    if padded > key_count:
        pad = jnp.zeros((padded - key_count, HEAD_DIM), jnp.bfloat16)
        for k in range(kv_used):
            keys_ref[k, key_count:, :] = pad
            values_ref[k, key_count:, :] = pad

    def wait(k):
        keys, values = copies(k)
        keys.wait()
        if k == 0:
            for later in range(1, kv_used):
                for copy in copies(later):
                    copy.start()
        return values.wait

    attend_block(
        q_ref, keys_ref, values_ref, out_ref, lse_ref, scores_sc, key_count, wait
    )


def attend_own(where, packed, image_kv, kv_used, q_rows, with_lse):
    _, tile_len, tiles_dev, _ = image_kv.shape
    padded = -(-tile_len * tiles_dev // 16) * 16
    held = pltpu.VMEM((kv_used, padded, HEAD_DIM), jnp.bfloat16)
    out_shape = [pltpu.VMEM((q_rows, HEAD_DIM), jnp.bfloat16)]
    if with_lse:
        out_shape.append(pltpu.VMEM((q_rows, HEAD_DIM), jnp.float32))
    out_shape += [held, held]
    results = pl.pallas_call(
        functools.partial(own_body, with_lse=with_lse),
        out_shape=out_shape,
        in_specs=[SMEM, VMEM, HBM],
        out_specs=[VMEM] * len(out_shape),
        scratch_shapes=[
            pltpu.VMEM((q_rows // kv_used, padded), jnp.float32),
            pltpu.SemaphoreType.DMA((2, kv_used)),
        ],
        compiler_params=PARAMS,
        name="attend_own",
    )(where, in_vmem(packed), in_hbm(image_kv))
    return results[:-2], [in_vmem(part) for part in results[-2:]]


def arrived_body(q_ref, keys_ref, values_ref, out_ref, *refs, with_lse, key_count):
    lse_ref = refs[0] if with_lse else None
    attend_block(
        q_ref, keys_ref, values_ref, out_ref, lse_ref, refs[-1], key_count, no_wait
    )


def attend_arrived(packed, held, key_count, q_rows, with_lse):
    kv_used, padded, _ = held[0].shape
    out_shape = [pltpu.VMEM((q_rows, HEAD_DIM), jnp.bfloat16)]
    if with_lse:
        out_shape.append(pltpu.VMEM((q_rows, HEAD_DIM), jnp.float32))
    return pl.pallas_call(
        functools.partial(arrived_body, with_lse=with_lse, key_count=key_count),
        out_shape=out_shape,
        in_specs=[VMEM] * 3,
        out_specs=[VMEM] * len(out_shape),
        scratch_shapes=[pltpu.VMEM((q_rows // kv_used, padded), jnp.float32)],
        compiler_params=PARAMS,
        name="attend_arrived",
    )(in_vmem(packed), *held)


def join_body(partial_ref, message_ref, out_ref):
    q_rows = partial_ref.shape[0]
    out_ref[:q_rows, :] = partial_ref[...]
    out_ref[q_rows:, :] = message_ref[q_rows : out_ref.shape[0], :]


def join_keys(partial, message):
    return pl.pallas_call(
        join_body,
        out_shape=pltpu.VMEM((message.shape[0] - META_ROWS, HEAD_DIM), jnp.bfloat16),
        in_specs=[VMEM] * 2,
        out_specs=VMEM,
        compiler_params=PARAMS,
        name="join_keys",
    )(in_vmem(partial), in_vmem(message))


def self_body(where_ref, docs_ref, q_ref, *refs, starts, kv_used):
    kv_refs, out_ref, bias_sc = refs[:-2], refs[-2], refs[-1]
    tok_rows, q_width = q_ref.shape
    per_kv = q_width // HEAD_DIM // kv_used
    shape = bias_sc.shape
    row_start = where_ref[0] * tok_rows
    query_pos = row_start + lax.broadcasted_iota(jnp.int32, (tok_rows, 1), 0)
    key_pos = row_start + tok_rows - shape[1] + lax.broadcasted_iota(jnp.int32, shape, 1)
    doc_start = jnp.zeros((tok_rows, 1), jnp.int32)
    doc_end = jnp.int32(0)
    for j in range(docs_ref.shape[0]):
        doc_end = doc_end + docs_ref[j]
        doc_start = jnp.where(query_pos >= doc_end, doc_end, doc_start)
    bias_sc[...] = jnp.where((key_pos <= query_pos) & (key_pos >= doc_start), 0.0, NEG_FILL)
    for k in range(kv_used):
        keys, values = [
            jnp.concatenate(
                [
                    ref[at + (w * kv_used + k) * tok_rows : at + (w * kv_used + k + 1) * tok_rows, :]
                    for ref, at in zip(kv_refs, starts)
                ],
                axis=0,
            )
            for w in range(2)
        ]
        heads = range(k * per_kv, (k + 1) * per_kv)
        q = jnp.concatenate([q_ref[:, h * HEAD_DIM : (h + 1) * HEAD_DIM] for h in heads], axis=0)
        scores = lax.dot_general(
            q, keys, (((1,), (1,)), ((), ())), preferred_element_type=jnp.float32
        )
        scores = scores * EXP2_SCALE + jnp.concatenate([bias_sc[...]] * per_kv, axis=0)
        row_best = jnp.max(scores, axis=1, keepdims=True)
        weights = jnp.exp2(scores - row_best)
        row_total = jnp.sum(weights, axis=1, keepdims=True)
        blended = jnp.dot(weights.astype(jnp.bfloat16), values, preferred_element_type=jnp.float32)
        blended = blended / row_total
        for i, h in enumerate(heads):
            out_ref[:, h * HEAD_DIM : (h + 1) * HEAD_DIM] = blended[i * tok_rows : (i + 1) * tok_rows]


def attend_self(where, doc_lengths, q_self, pieces, kv_used):
    tok_rows, q_width = q_self.shape
    return pl.pallas_call(
        functools.partial(self_body, starts=[at for _, at in pieces], kv_used=kv_used),
        out_shape=pltpu.VMEM((tok_rows, q_width), jnp.float32),
        in_specs=[SMEM, SMEM] + [VMEM] * (1 + len(pieces)),
        out_specs=VMEM,
        scratch_shapes=[pltpu.VMEM((tok_rows, len(pieces) * tok_rows), jnp.float32)],
        compiler_params=PARAMS,
        name="attend_self",
    )(where, doc_lengths, in_vmem(q_self), *[in_vmem(array) for array, _ in pieces])


def mix_blocks(blocks_ref, gate_ref, self_ref, partial_refs, distances, out_hbm, out_ref, sem):
    copies = []
    for i, (distance, partial_ref) in enumerate(zip(distances, partial_refs)):
        rows = pl.ds(pl.multiple_of(blocks_ref[distance] * BLOCK, BLOCK), BLOCK)
        for h in range(self_ref.shape[1] // HEAD_DIM):
            cols = slice(h * HEAD_DIM, (h + 1) * HEAD_DIM)
            cross = partial_ref[h * BLOCK : (h + 1) * BLOCK, :].astype(jnp.float32)
            mixed = self_ref[rows, cols] + gate_ref[:, cols] * cross
            out_ref[i, :, cols] = mixed.astype(jnp.bfloat16)
        copy = pltpu.make_async_copy(out_ref.at[i], out_hbm.at[rows, :], sem.at[i])
        copy.start()
        copies.append(copy)
    for copy in copies:
        copy.wait()


def early_body(pairs_ref, slots_ref, gate_ref, self_ref, *refs, distances, tiles_dev):
    partial_refs, (out_hbm, blocks_ref, out_ref, sem) = refs[:-4], refs[-4:]
    stored = owner_slots(pairs_ref, slots_ref)
    here = lax.axis_index("ctx")
    ctx_count = blocks_ref.shape[0]
    for distance in range(ctx_count):
        owner = lax.rem(here + distance, ctx_count)
        blocks_ref[distance] = block_for(stored, owner, tiles_dev)[0]
    mix_blocks(blocks_ref, gate_ref, self_ref, partial_refs, distances, out_hbm, out_ref, sem)


def late_body(blocks_ref, gate_ref, self_ref, *refs, distances):
    partial_refs, (_, out_hbm, out_ref, sem) = refs[:-4], refs[-4:]
    mix_blocks(blocks_ref, gate_ref, self_ref, partial_refs, distances, out_hbm, out_ref, sem)


def mix(pair_tiles, tile_slot, gate_cols, self_out, partials, tiles_dev):
    ctx_count = len(partials)
    early, late = [0, ctx_count - 1], list(range(1, ctx_count - 1))
    out_shape = jax.ShapeDtypeStruct(self_out.shape, jnp.bfloat16)

    def scratch(distances):
        return [
            pltpu.VMEM((len(distances), BLOCK, self_out.shape[1]), jnp.bfloat16),
            pltpu.SemaphoreType.DMA((len(distances),)),
        ]

    shared = (in_vmem(gate_cols), in_vmem(self_out))
    out, blocks = pl.pallas_call(
        functools.partial(early_body, distances=early, tiles_dev=tiles_dev),
        out_shape=[out_shape, pltpu.SMEM((ctx_count,), jnp.int32)],
        in_specs=[SMEM] * 2 + [VMEM] * (2 + len(early)),
        out_specs=[HBM, SMEM],
        scratch_shapes=scratch(early),
        compiler_params=PARAMS,
        name="mix_early",
    )(pair_tiles, tile_slot, *shared, *[in_vmem(partials[d]) for d in early])
    return pl.pallas_call(
        functools.partial(late_body, distances=late),
        out_shape=out_shape,
        in_specs=[SMEM] + [VMEM] * (2 + len(late)) + [HBM],
        out_specs=HBM,
        scratch_shapes=scratch(late),
        input_output_aliases={3 + len(late): 0},
        compiler_params=PARAMS,
        name="mix_late",
    )(
        pltpu.with_memory_space_constraint(blocks, pltpu.SMEM),
        *shared,
        *[in_vmem(partials[d]) for d in late],
        in_hbm(out),
    )


def mix_owners(where, pair_tiles, tile_slot, gate_cols, self_out, partials, sums, tiles_dev):
    block_count = pair_tiles.shape[0]
    tok_rows, q_width = self_out.shape
    heads = q_width // HEAD_DIM
    ctx_count = len(partials)
    owners = jnp.take(tile_slot, pair_tiles.reshape(-1), axis=0).reshape(block_count, -1) // tiles_dev
    partners = (where[0] + jnp.arange(ctx_count, dtype=jnp.int32)) % ctx_count
    live = jnp.any(owners[:, :, None] == partners[None, None, :], axis=1)[:, :, None, None]
    lse = jnp.stack(sums)[None]
    top = jnp.max(jnp.where(live, lse, NEG_FILL), axis=1, keepdims=True)
    factors = jnp.where(live, jnp.exp(lse - top), 0.0)
    pieces = jnp.stack(partials).astype(jnp.float32)[None]
    cross = jnp.sum(factors * pieces, axis=1) / jnp.sum(factors, axis=1)
    cross = jnp.transpose(cross.reshape(block_count, heads, BLOCK, HEAD_DIM), (0, 2, 1, 3))
    return (self_out + gate_cols * cross.reshape(tok_rows, q_width)).astype(jnp.bfloat16)


def partner_order(ctx_count):
    return list(range(ctx_count - 1, 0, -1))


def attend(q_self, q_cross, kv_self, image_kv, cross_gate, doc_lengths, pair_tiles, tile_slot):
    tok_rows, q_width = q_self.shape
    local_heads = q_width // HEAD_DIM
    q_rows = local_heads * BLOCK
    grouping = Q_HEADS // KV_HEADS
    per_kv = min(local_heads, grouping)
    kv_used = local_heads // per_kv
    ctx_count = lax.axis_size("ctx")
    tiles_dev, tile_len = image_kv.shape[1:3]
    request_count = pair_tiles.shape[0] * PAIRS
    capacity = max(2, -(-request_count // ctx_count))
    one_owner = ctx_count * capacity == request_count and capacity == PAIRS
    with_lse = not one_owner
    reach = min(ctx_count - 1, -(-(ctx_count * tok_rows // 2 - 1) // tok_rows))

    here = lax.axis_index("ctx").astype(jnp.int32)

    def kv_first():
        return lax.axis_index("rep") * local_heads // grouping

    where = jnp.stack([here, kv_first().astype(jnp.int32)])
    image_kv = jnp.transpose(image_kv, (0, 2, 1, 3))

    def send(array, distance):
        pairs = [(i, (i + distance) % ctx_count) for i in range(ctx_count)]
        return lax.ppermute(array, "ctx", pairs)

    packed = pack_queries(
        pair_tiles, tile_slot, q_cross, kv_self, ctx_count, tiles_dev, kv_used, kv_first
    )
    last = ctx_count - 1
    order = partner_order(ctx_count)
    arrived = {d: send(packed[d], d) for d in order[-1:] + order[:-1]}
    results = {}
    results[0], held = attend_own(where, packed[0], image_kv, kv_used, q_rows, with_lse)
    for d in order:
        answer = attend_arrived(arrived[d], held, tile_len * tiles_dev, q_rows, with_lse)
        if d == last:
            answer = [join_keys(answer[0], arrived[1]), *answer[1:]]
        results[d] = [send(part, ctx_count - d) for part in answer]

    pieces = [packed[1], arrived[1], results[last][0]][: reach + 1]
    pieces = [(piece, q_rows) for piece in pieces]
    for _ in range(len(pieces), reach + 1):
        array, first = pieces[-1]
        rows = 2 * kv_used * tok_rows
        pieces.append((send(array[first : first + rows], 1), 0))
    self_out = attend_self(where, doc_lengths, q_self, pieces[::-1], kv_used)
    gate_cols = jnp.repeat(jnp.tanh(cross_gate), HEAD_DIM)[None, :]
    partials = [results[d][0] for d in range(ctx_count)]
    if one_owner:
        return mix(pair_tiles, tile_slot, gate_cols, self_out, partials, tiles_dev)
    partials = [partial[:q_rows] for partial in partials]
    sums = [results[d][1] for d in range(ctx_count)]
    return mix_owners(where, pair_tiles, tile_slot, gate_cols, self_out, partials, sums, tiles_dev)


def solution(mesh):
    in_specs = (
        P(("groups", "ctx"), ("head", "rep")),
        P(("groups", "ctx"), ("head", "rep")),
        P(None, ("groups", "ctx"), "head"),
        P(None, ("groups", "ctx"), None, "head"),
        P(("head", "rep")),
        P("groups"),
        P(("groups", "ctx"), None),
        P("groups"),
    )
    out_specs = P(("groups", "ctx"), ("head", "rep"))
    return jax.shard_map(attend, mesh=mesh, in_specs=in_specs, out_specs=out_specs, check_vma=False)
```

```python
import functools
import math

import jax
import jax.numpy as jnp
from jax import lax
from jax.experimental import pallas as pl
from jax.experimental.pallas import tpu as pltpu
from jax.sharding import PartitionSpec as P


HEAD_DIM = 128
Q_HEADS = 64
KV_HEADS = 8
BLOCK = 32
PAIRS = 4

NEG_FILL = -1e30
META_ROWS = 8
KEY_CHUNK = 256
LAG = 2
MOST_TOTAL = 2.0**100
LOG2E = math.log2(math.e)
EXP2_SCALE = HEAD_DIM ** (-0.5) * LOG2E

SMEM = pl.BlockSpec(memory_space=pltpu.SMEM)
VMEM = pl.BlockSpec(memory_space=pltpu.VMEM)
HBM = pl.BlockSpec(memory_space=pltpu.HBM)
PARAMS = pltpu.CompilerParams(vmem_limit_bytes=24 << 20)


def in_vmem(array):
    return pltpu.with_memory_space_constraint(array, pltpu.VMEM)


def in_hbm(array):
    return pltpu.with_memory_space_constraint(array, pltpu.HBM)


def owner_slots(pairs_ref, slots_ref):
    blocks, pairs = pairs_ref.shape
    return [[slots_ref[pairs_ref[b, p]] for p in range(pairs)] for b in range(blocks)]


def block_for(stored, owner, tiles_dev):
    block = jnp.int32(0)
    counts = [jnp.int32(0)] * tiles_dev
    for b, row in enumerate(stored):
        for slot in row:
            tile = slot - owner * tiles_dev
            block = jnp.where((tile >= 0) & (tile < tiles_dev), jnp.int32(b), block)
            counts = [n + (tile == i).astype(jnp.int32) for i, n in enumerate(counts)]
    return block, counts


def pack_body(
    pairs_hbm, slots_hbm, q_hbm, kv_hbm, *refs, tiles_dev, kv_used, kv_first
):
    out_refs = refs[:-5]
    q_ref, pairs_ref, slots_ref, kv_sem, sem = refs[-5:]
    ctx_count = len(out_refs)
    heads = q_ref.shape[1] // HEAD_DIM
    tok_rows = kv_hbm.shape[1]
    kv_at = heads * BLOCK
    tables = [
        pltpu.make_async_copy(pairs_hbm, pairs_ref, sem.at[0]),
        pltpu.make_async_copy(slots_hbm, slots_ref, sem.at[1]),
    ]
    queries = pltpu.make_async_copy(q_hbm, q_ref, sem.at[2])
    copies = []
    for w in range(2):
        for k in range(kv_used):
            cols = pl.ds(pl.multiple_of((kv_first() + k) * HEAD_DIM, HEAD_DIM), HEAD_DIM)
            part = w * kv_used + k
            rows = pl.ds(kv_at + part * tok_rows, tok_rows)
            copies.append(
                pltpu.make_async_copy(kv_hbm.at[w, :, cols], out_refs[1].at[rows, :], kv_sem.at[part])
            )
    for copy in tables + [queries] + copies:
        copy.start()
    for copy in tables:
        copy.wait()
    stored = owner_slots(pairs_ref, slots_ref)
    here = lax.axis_index("ctx")
    lanes = lax.broadcasted_iota(jnp.int32, (META_ROWS, HEAD_DIM), 1)
    blocks = []
    for distance, out_ref in enumerate(out_refs):
        owner = lax.rem(here + distance, ctx_count)
        block, counts = block_for(stored, owner, tiles_dev)
        blocks.append(block)
        meta = jnp.zeros((META_ROWS, HEAD_DIM), jnp.float32)
        for i, n in enumerate(counts):
            meta = jnp.where(lanes % tiles_dev == i, n.astype(jnp.float32), meta)
        out_ref[out_ref.shape[0] - META_ROWS :, :] = meta.astype(jnp.bfloat16)
    queries.wait()
    for block, out_ref in zip(blocks, out_refs):
        rows = pl.ds(pl.multiple_of(block * BLOCK, BLOCK), BLOCK)
        for h in range(heads):
            out_ref[h * BLOCK : (h + 1) * BLOCK, :] = q_ref[rows, h * HEAD_DIM : (h + 1) * HEAD_DIM]
    for copy in copies:
        copy.wait()


def pack_queries(pair_tiles, tile_slot, q_cross, kv_self, ctx_count, tiles_dev, kv_used, kv_first):
    rows = q_cross.shape[1] // HEAD_DIM * BLOCK + META_ROWS
    kv_rows = 2 * kv_used * kv_self.shape[1]
    return pl.pallas_call(
        functools.partial(pack_body, tiles_dev=tiles_dev, kv_used=kv_used, kv_first=kv_first),
        out_shape=[
            pltpu.VMEM((rows + (kv_rows if d == 1 else 0), HEAD_DIM), jnp.bfloat16)
            for d in range(ctx_count)
        ],
        in_specs=[HBM] * 4,
        out_specs=[VMEM] * ctx_count,
        scratch_shapes=[
            pltpu.VMEM(q_cross.shape, q_cross.dtype),
            pltpu.SMEM(pair_tiles.shape, jnp.int32),
            pltpu.SMEM(tile_slot.shape, jnp.int32),
            pltpu.SemaphoreType.DMA((2 * kv_used,)),
            pltpu.SemaphoreType.DMA((3,)),
        ],
        compiler_params=PARAMS,
        name="pack_queries",
    )(in_hbm(pair_tiles), in_hbm(tile_slot), in_hbm(q_cross), in_hbm(kv_self))


def count_bias(meta):
    count = meta[0:1, :].astype(jnp.float32)
    return jnp.where(count > 0, jnp.log(jnp.maximum(count, 1.0)) * LOG2E, NEG_FILL)


def finish_head(blended, total, best):
    live = total > 0
    total = jnp.where(live, total, 1.0)
    out = (blended / total).astype(jnp.bfloat16)
    lse = jnp.where(live, best * (1.0 / LOG2E) + jnp.log(total), NEG_FILL)
    return out, jnp.broadcast_to(lse, (lse.shape[0], HEAD_DIM))


def attend_head(q, meta, keys, values, key_count, wait_values):
    rows = q.shape[0]
    padded = keys.shape[0]
    lanes = HEAD_DIM
    bias = count_bias(meta)

    def score(at, size):
        return lax.dot_general(
            q, keys[at : at + size, :], (((1,), (1,)), ((), ())), preferred_element_type=jnp.float32
        )

    first = score(0, KEY_CHUNK)
    best = first[:, :lanes]
    for col in range(lanes, KEY_CHUNK, lanes):
        best = jnp.maximum(best, first[:, col : col + lanes])
    best = jnp.max(best * EXP2_SCALE + bias, axis=1, keepdims=True)
    shift = jnp.where(best > 0.5 * NEG_FILL, bias - best, NEG_FILL)
    totals = jnp.zeros((rows, lanes), jnp.float32)
    total = jnp.zeros((rows, 1), jnp.float32)
    blended = jnp.zeros((rows, HEAD_DIM), jnp.float32)
    waiting = []
    wait_values()
    for at in list(range(0, padded, KEY_CHUNK)) + [None] * LAG:
        if at is not None:
            size = min(KEY_CHUNK, padded - at)
            scores = score(at, size)
            pieces = []
            for col in range(0, size, lanes):
                width = min(lanes, size - col)
                weights = jnp.exp2(scores[:, col : col + width] * EXP2_SCALE + shift[:, :width])
                valid = key_count - at - col
                if width > valid:
                    held = lax.broadcasted_iota(jnp.int32, weights.shape, 1) < valid
                    weights = jnp.where(held, weights, 0.0)
                if width == lanes:
                    totals = totals + weights
                else:
                    total = total + jnp.sum(weights, axis=1, keepdims=True)
                pieces.append(weights.astype(jnp.bfloat16))
            weights = jnp.concatenate(pieces, axis=1) if len(pieces) > 1 else pieces[0]
            waiting.append((weights, at))
        if len(waiting) > LAG or at is None:
            weights, start = waiting.pop(0)
            blended = blended + jnp.dot(
                weights,
                values[start : start + weights.shape[1], :],
                preferred_element_type=jnp.float32,
            )
    total = total + jnp.sum(totals, axis=1, keepdims=True)
    return *finish_head(blended, total, best), total


def attend_head_exact(q, meta, keys, values, key_count, scores_sc):
    rows = q.shape[0]
    padded = keys.shape[0]
    lanes = HEAD_DIM
    bias = count_bias(meta)
    best = None
    for at in range(0, padded, KEY_CHUNK):
        size = min(KEY_CHUNK, padded - at)
        scores = lax.dot_general(
            q, keys[at : at + size, :], (((1,), (1,)), ((), ())), preferred_element_type=jnp.float32
        )
        for col in range(0, size, lanes):
            width = min(lanes, size - col)
            piece = scores[:, col : col + width]
            valid = key_count - at - col
            if width > valid:
                piece = jnp.where(lax.broadcasted_iota(jnp.int32, piece.shape, 1) < valid, piece, NEG_FILL)
            scores_sc[:, at + col : at + col + width] = piece
            if width == lanes:
                best = piece if best is None else jnp.maximum(best, piece)
            else:
                tail = piece
    best = jnp.max(best * EXP2_SCALE + bias, axis=1, keepdims=True)
    tail_width = padded % lanes
    if tail_width:
        tail = jnp.max(tail * EXP2_SCALE + bias[:, :tail_width], axis=1, keepdims=True)
        best = jnp.maximum(best, tail)
    shift = jnp.where(best > 0.5 * NEG_FILL, bias - best, NEG_FILL)
    totals = jnp.zeros((rows, lanes), jnp.float32)
    total = jnp.zeros((rows, 1), jnp.float32)
    blended = jnp.zeros((rows, HEAD_DIM), jnp.float32)
    for at in range(0, padded, KEY_CHUNK):
        size = min(KEY_CHUNK, padded - at)
        pieces = []
        for col in range(0, size, lanes):
            width = min(lanes, size - col)
            piece = scores_sc[:, at + col : at + col + width]
            weights = jnp.exp2(piece * EXP2_SCALE + shift[:, :width])
            if width == lanes:
                totals = totals + weights
            else:
                total = total + jnp.sum(weights, axis=1, keepdims=True)
            pieces.append(weights.astype(jnp.bfloat16))
        weights = jnp.concatenate(pieces, axis=1) if len(pieces) > 1 else pieces[0]
        blended = blended + jnp.dot(
            weights, values[at : at + size, :], preferred_element_type=jnp.float32
        )
    total = total + jnp.sum(totals, axis=1, keepdims=True)
    return finish_head(blended, total, best)


def attend_block(q_ref, keys_ref, values_ref, out_ref, lse_ref, scores_sc, key_count, wait):
    kv_used = keys_ref.shape[0]
    rows = scores_sc.shape[0]
    meta = q_ref[q_ref.shape[0] - META_ROWS :, :]

    def place(k):
        return slice(k * rows, (k + 1) * rows)

    def store(k, out, lse):
        out_ref[place(k), :] = out
        if lse_ref is not None:
            lse_ref[place(k), :] = lse

    highest = jnp.zeros((rows, 1), jnp.float32)
    for k in range(kv_used):
        wait_values = wait(k)
        keys, values = keys_ref.at[k], values_ref.at[k]
        out, lse, total = attend_head(q_ref[place(k), :], meta, keys, values, key_count, wait_values)
        store(k, out, lse)
        highest = jnp.maximum(highest, total)

    @pl.when(jnp.logical_not(jnp.max(highest) <= MOST_TOTAL))
    def _():
        for k in range(kv_used):
            keys, values = keys_ref.at[k], values_ref.at[k]
            store(
                k,
                *attend_head_exact(q_ref[place(k), :], meta, keys, values, key_count, scores_sc),
            )


def no_wait(k):
    return lambda: None


def own_body(q_ref, image_hbm, *refs, with_lse, kv_first):
    out_ref = refs[0]
    lse_ref = refs[1] if with_lse else None
    keys_ref, values_ref, scores_sc, sem = refs[-4:]
    _, tile_len, tiles_dev, width = image_hbm.shape
    key_count = tile_len * tiles_dev
    kv_used, padded = keys_ref.shape[:2]
    image = image_hbm.reshape(2, key_count, width)

    def copies(k):
        cols = pl.ds(pl.multiple_of((kv_first() + k) * HEAD_DIM, HEAD_DIM), HEAD_DIM)
        held = pl.ds(0, key_count)
        return [
            pltpu.make_async_copy(image.at[w, :, cols], ref.at[k, held], sem.at[w, k])
            for w, ref in enumerate((keys_ref, values_ref))
        ]

    if padded > key_count:
        pad = jnp.zeros((padded - key_count, HEAD_DIM), jnp.bfloat16)
        for k in range(kv_used):
            keys_ref[k, key_count:, :] = pad
            values_ref[k, key_count:, :] = pad
    for copy in copies(0):
        copy.start()

    def wait(k):
        keys, values = copies(k)
        keys.wait()
        if k == 0:
            for later in range(1, kv_used):
                for copy in copies(later):
                    copy.start()
        return values.wait

    attend_block(
        q_ref, keys_ref, values_ref, out_ref, lse_ref, scores_sc, key_count, wait
    )


def attend_own(packed, image_kv, kv_used, q_rows, with_lse, kv_first):
    _, tile_len, tiles_dev, _ = image_kv.shape
    padded = -(-tile_len * tiles_dev // 16) * 16
    held = pltpu.VMEM((kv_used, padded, HEAD_DIM), jnp.bfloat16)
    out_shape = [pltpu.VMEM((q_rows, HEAD_DIM), jnp.bfloat16)]
    if with_lse:
        out_shape.append(pltpu.VMEM((q_rows, HEAD_DIM), jnp.float32))
    out_shape += [held, held]
    results = pl.pallas_call(
        functools.partial(own_body, with_lse=with_lse, kv_first=kv_first),
        out_shape=out_shape,
        in_specs=[VMEM, HBM],
        out_specs=[VMEM] * len(out_shape),
        scratch_shapes=[
            pltpu.VMEM((q_rows // kv_used, padded), jnp.float32),
            pltpu.SemaphoreType.DMA((2, kv_used)),
        ],
        compiler_params=PARAMS,
        name="attend_own",
    )(in_vmem(packed), in_hbm(image_kv))
    return results[:-2], [in_vmem(part) for part in results[-2:]]


def arrived_body(q_ref, keys_ref, values_ref, out_ref, *refs, with_lse, key_count):
    lse_ref = refs[0] if with_lse else None
    attend_block(
        q_ref, keys_ref, values_ref, out_ref, lse_ref, refs[-1], key_count, no_wait
    )


def attend_arrived(packed, held, key_count, q_rows, with_lse):
    kv_used, padded, _ = held[0].shape
    out_shape = [pltpu.VMEM((q_rows, HEAD_DIM), jnp.bfloat16)]
    if with_lse:
        out_shape.append(pltpu.VMEM((q_rows, HEAD_DIM), jnp.float32))
    return pl.pallas_call(
        functools.partial(arrived_body, with_lse=with_lse, key_count=key_count),
        out_shape=out_shape,
        in_specs=[VMEM] * 3,
        out_specs=[VMEM] * len(out_shape),
        scratch_shapes=[pltpu.VMEM((q_rows // kv_used, padded), jnp.float32)],
        compiler_params=PARAMS,
        name="attend_arrived",
    )(in_vmem(packed), *held)


def join_body(partial_ref, message_ref, out_ref):
    q_rows = partial_ref.shape[0]
    out_ref[:q_rows, :] = partial_ref[...]
    out_ref[q_rows:, :] = message_ref[q_rows : out_ref.shape[0], :]


def join_keys(partial, message):
    return pl.pallas_call(
        join_body,
        out_shape=pltpu.VMEM((message.shape[0] - META_ROWS, HEAD_DIM), jnp.bfloat16),
        in_specs=[VMEM] * 2,
        out_specs=VMEM,
        compiler_params=PARAMS,
        name="join_keys",
    )(in_vmem(partial), in_vmem(message))


def self_body(docs_ref, q_ref, *refs, starts, kv_used):
    kv_refs, out_ref, bias_sc = refs[:-2], refs[-2], refs[-1]
    tok_rows, q_width = q_ref.shape
    per_kv = q_width // HEAD_DIM // kv_used
    shape = bias_sc.shape
    row_start = lax.axis_index("ctx") * tok_rows
    query_pos = row_start + lax.broadcasted_iota(jnp.int32, (tok_rows, 1), 0)
    key_pos = row_start + tok_rows - shape[1] + lax.broadcasted_iota(jnp.int32, shape, 1)
    doc_start = jnp.zeros((tok_rows, 1), jnp.int32)
    doc_end = jnp.int32(0)
    for j in range(docs_ref.shape[0]):
        doc_end = doc_end + docs_ref[j]
        doc_start = jnp.where(query_pos >= doc_end, doc_end, doc_start)
    bias_sc[...] = jnp.where((key_pos <= query_pos) & (key_pos >= doc_start), 0.0, NEG_FILL)
    for k in range(kv_used):
        keys, values = [
            jnp.concatenate(
                [
                    ref[at + (w * kv_used + k) * tok_rows : at + (w * kv_used + k + 1) * tok_rows, :]
                    for ref, at in zip(kv_refs, starts)
                ],
                axis=0,
            )
            for w in range(2)
        ]
        heads = range(k * per_kv, (k + 1) * per_kv)
        q = jnp.concatenate([q_ref[:, h * HEAD_DIM : (h + 1) * HEAD_DIM] for h in heads], axis=0)
        scores = lax.dot_general(
            q, keys, (((1,), (1,)), ((), ())), preferred_element_type=jnp.float32
        )
        scores = scores * EXP2_SCALE + jnp.concatenate([bias_sc[...]] * per_kv, axis=0)
        row_best = jnp.max(scores, axis=1, keepdims=True)
        weights = jnp.exp2(scores - row_best)
        row_total = jnp.sum(weights, axis=1, keepdims=True)
        blended = jnp.dot(weights.astype(jnp.bfloat16), values, preferred_element_type=jnp.float32)
        blended = blended / row_total
        for i, h in enumerate(heads):
            out_ref[:, h * HEAD_DIM : (h + 1) * HEAD_DIM] = blended[i * tok_rows : (i + 1) * tok_rows]


def attend_self(doc_lengths, q_self, pieces, kv_used):
    tok_rows, q_width = q_self.shape
    return pl.pallas_call(
        functools.partial(self_body, starts=[at for _, at in pieces], kv_used=kv_used),
        out_shape=pltpu.VMEM((tok_rows, q_width), jnp.float32),
        in_specs=[SMEM] + [VMEM] * (1 + len(pieces)),
        out_specs=VMEM,
        scratch_shapes=[pltpu.VMEM((tok_rows, len(pieces) * tok_rows), jnp.float32)],
        compiler_params=PARAMS,
        name="attend_self",
    )(doc_lengths, in_vmem(q_self), *[in_vmem(array) for array, _ in pieces])


def mix_blocks(blocks_ref, gate_ref, self_ref, partial_refs, distances, out_hbm, out_ref, sem):
    copies = []
    for i, (distance, partial_ref) in enumerate(zip(distances, partial_refs)):
        rows = pl.ds(pl.multiple_of(blocks_ref[distance] * BLOCK, BLOCK), BLOCK)
        for h in range(self_ref.shape[1] // HEAD_DIM):
            cols = slice(h * HEAD_DIM, (h + 1) * HEAD_DIM)
            cross = partial_ref[h * BLOCK : (h + 1) * BLOCK, :].astype(jnp.float32)
            mixed = self_ref[rows, cols] + gate_ref[:, cols] * cross
            out_ref[i, :, cols] = mixed.astype(jnp.bfloat16)
        copy = pltpu.make_async_copy(out_ref.at[i], out_hbm.at[rows, :], sem.at[i])
        copy.start()
        copies.append(copy)
    for copy in copies:
        copy.wait()


def early_body(pairs_ref, slots_ref, gate_ref, self_ref, *refs, distances, tiles_dev):
    partial_refs, (out_hbm, blocks_ref, out_ref, sem) = refs[:-4], refs[-4:]
    stored = owner_slots(pairs_ref, slots_ref)
    here = lax.axis_index("ctx")
    ctx_count = blocks_ref.shape[0]
    for distance in range(ctx_count):
        owner = lax.rem(here + distance, ctx_count)
        blocks_ref[distance] = block_for(stored, owner, tiles_dev)[0]
    mix_blocks(blocks_ref, gate_ref, self_ref, partial_refs, distances, out_hbm, out_ref, sem)


def late_body(blocks_ref, gate_ref, self_ref, *refs, distances):
    partial_refs, (_, out_hbm, out_ref, sem) = refs[:-4], refs[-4:]
    mix_blocks(blocks_ref, gate_ref, self_ref, partial_refs, distances, out_hbm, out_ref, sem)


def mix(pair_tiles, tile_slot, gate_cols, self_out, partials, tiles_dev):
    ctx_count = len(partials)
    early, late = [0, ctx_count - 1], list(range(1, ctx_count - 1))
    out_shape = jax.ShapeDtypeStruct(self_out.shape, jnp.bfloat16)

    def scratch(distances):
        return [
            pltpu.VMEM((len(distances), BLOCK, self_out.shape[1]), jnp.bfloat16),
            pltpu.SemaphoreType.DMA((len(distances),)),
        ]

    shared = (in_vmem(gate_cols), in_vmem(self_out))
    out, blocks = pl.pallas_call(
        functools.partial(early_body, distances=early, tiles_dev=tiles_dev),
        out_shape=[out_shape, pltpu.SMEM((ctx_count,), jnp.int32)],
        in_specs=[SMEM] * 2 + [VMEM] * (2 + len(early)),
        out_specs=[HBM, SMEM],
        scratch_shapes=scratch(early),
        compiler_params=PARAMS,
        name="mix_early",
    )(pair_tiles, tile_slot, *shared, *[in_vmem(partials[d]) for d in early])
    return pl.pallas_call(
        functools.partial(late_body, distances=late),
        out_shape=out_shape,
        in_specs=[SMEM] + [VMEM] * (2 + len(late)) + [HBM],
        out_specs=HBM,
        scratch_shapes=scratch(late),
        input_output_aliases={3 + len(late): 0},
        compiler_params=PARAMS,
        name="mix_late",
    )(
        pltpu.with_memory_space_constraint(blocks, pltpu.SMEM),
        *shared,
        *[in_vmem(partials[d]) for d in late],
        in_hbm(out),
    )


def mix_owners(pair_tiles, tile_slot, gate_cols, self_out, partials, sums, tiles_dev):
    block_count = pair_tiles.shape[0]
    tok_rows, q_width = self_out.shape
    heads = q_width // HEAD_DIM
    ctx_count = len(partials)
    owners = jnp.take(tile_slot, pair_tiles.reshape(-1), axis=0).reshape(block_count, -1) // tiles_dev
    partners = (lax.axis_index("ctx") + jnp.arange(ctx_count, dtype=jnp.int32)) % ctx_count
    live = jnp.any(owners[:, :, None] == partners[None, None, :], axis=1)[:, :, None, None]
    lse = jnp.stack(sums)[None]
    top = jnp.max(jnp.where(live, lse, NEG_FILL), axis=1, keepdims=True)
    factors = jnp.where(live, jnp.exp(lse - top), 0.0)
    pieces = jnp.stack(partials).astype(jnp.float32)[None]
    cross = jnp.sum(factors * pieces, axis=1) / jnp.sum(factors, axis=1)
    cross = jnp.transpose(cross.reshape(block_count, heads, BLOCK, HEAD_DIM), (0, 2, 1, 3))
    return (self_out + gate_cols * cross.reshape(tok_rows, q_width)).astype(jnp.bfloat16)


def partner_order(ctx_count):
    return list(range(ctx_count - 1, 0, -1))


def attend(q_self, q_cross, kv_self, image_kv, cross_gate, doc_lengths, pair_tiles, tile_slot):
    tok_rows, q_width = q_self.shape
    local_heads = q_width // HEAD_DIM
    q_rows = local_heads * BLOCK
    grouping = Q_HEADS // KV_HEADS
    per_kv = min(local_heads, grouping)
    kv_used = local_heads // per_kv
    ctx_count = lax.axis_size("ctx")
    tiles_dev, tile_len = image_kv.shape[1:3]
    request_count = pair_tiles.shape[0] * PAIRS
    capacity = max(2, -(-request_count // ctx_count))
    one_owner = ctx_count * capacity == request_count and capacity == PAIRS
    with_lse = not one_owner
    reach = min(ctx_count - 1, -(-(ctx_count * tok_rows // 2 - 1) // tok_rows))


    def kv_first():
        return lax.axis_index("rep") * local_heads // grouping

    image_kv = jnp.transpose(image_kv, (0, 2, 1, 3))

    def send(array, distance):
        pairs = [(i, (i + distance) % ctx_count) for i in range(ctx_count)]
        return lax.ppermute(array, "ctx", pairs)

    packed = pack_queries(
        pair_tiles, tile_slot, q_cross, kv_self, ctx_count, tiles_dev, kv_used, kv_first
    )
    last = ctx_count - 1
    order = partner_order(ctx_count)
    arrived = {d: send(packed[d], d) for d in order[-1:] + order[:-1]}
    results = {}
    results[0], held = attend_own(packed[0], image_kv, kv_used, q_rows, with_lse, kv_first)
    for d in order:
        answer = attend_arrived(arrived[d], held, tile_len * tiles_dev, q_rows, with_lse)
        if d == last:
            answer = [join_keys(answer[0], arrived[1]), *answer[1:]]
        results[d] = [send(part, ctx_count - d) for part in answer]

    pieces = [packed[1], arrived[1], results[last][0]][: reach + 1]
    pieces = [(piece, q_rows) for piece in pieces]
    for _ in range(len(pieces), reach + 1):
        array, first = pieces[-1]
        rows = 2 * kv_used * tok_rows
        pieces.append((send(array[first : first + rows], 1), 0))
    self_out = attend_self(doc_lengths, q_self, pieces[::-1], kv_used)
    gate_cols = jnp.repeat(jnp.tanh(cross_gate), HEAD_DIM)[None, :]
    partials = [results[d][0] for d in range(ctx_count)]
    if one_owner:
        return mix(pair_tiles, tile_slot, gate_cols, self_out, partials, tiles_dev)
    partials = [partial[:q_rows] for partial in partials]
    sums = [results[d][1] for d in range(ctx_count)]
    return mix_owners(pair_tiles, tile_slot, gate_cols, self_out, partials, sums, tiles_dev)


def solution(mesh):
    in_specs = (
        P(("groups", "ctx"), ("head", "rep")),
        P(("groups", "ctx"), ("head", "rep")),
        P(None, ("groups", "ctx"), "head"),
        P(None, ("groups", "ctx"), None, "head"),
        P(("head", "rep")),
        P("groups"),
        P(("groups", "ctx"), None),
        P("groups"),
    )
    out_specs = P(("groups", "ctx"), ("head", "rep"))
    return jax.shard_map(attend, mesh=mesh, in_specs=in_specs, out_specs=out_specs, check_vma=False)
```

```python
import functools
import math

import jax
import jax.numpy as jnp
from jax import lax
from jax.experimental import pallas as pl
from jax.experimental.pallas import tpu as pltpu
from jax.sharding import PartitionSpec as P


HEAD_DIM = 128
Q_HEADS = 64
KV_HEADS = 8
BLOCK = 32
PAIRS = 4

NEG_FILL = -1e30
META_ROWS = 8
KEY_CHUNK = 256
LAG = 2
MOST_TOTAL = 2.0**100
LOG2E = math.log2(math.e)
EXP2_SCALE = HEAD_DIM ** (-0.5) * LOG2E

SMEM = pl.BlockSpec(memory_space=pltpu.SMEM)
VMEM = pl.BlockSpec(memory_space=pltpu.VMEM)
HBM = pl.BlockSpec(memory_space=pltpu.HBM)
PARAMS = pltpu.CompilerParams(vmem_limit_bytes=24 << 20)


def in_vmem(array):
    return pltpu.with_memory_space_constraint(array, pltpu.VMEM)


def in_hbm(array):
    return pltpu.with_memory_space_constraint(array, pltpu.HBM)


def owner_slots(pairs_ref, slots_ref):
    blocks, pairs = pairs_ref.shape
    return [[slots_ref[pairs_ref[b, p]] for p in range(pairs)] for b in range(blocks)]


def block_for(stored, owner, tiles_dev):
    block = jnp.int32(0)
    counts = [jnp.int32(0)] * tiles_dev
    for b, row in enumerate(stored):
        for slot in row:
            tile = slot - owner * tiles_dev
            block = jnp.where((tile >= 0) & (tile < tiles_dev), jnp.int32(b), block)
            counts = [n + (tile == i).astype(jnp.int32) for i, n in enumerate(counts)]
    return block, counts


def pack_body(
    pairs_hbm, slots_hbm, q_hbm, kv_hbm, *refs, tiles_dev, kv_used, kv_first
):
    out_refs = refs[:-5]
    q_ref, pairs_ref, slots_ref, kv_sem, sem = refs[-5:]
    ctx_count = len(out_refs)
    heads = q_ref.shape[1] // HEAD_DIM
    tok_rows = kv_hbm.shape[1]
    kv_at = heads * BLOCK
    tables = [
        pltpu.make_async_copy(pairs_hbm, pairs_ref, sem.at[0]),
        pltpu.make_async_copy(slots_hbm, slots_ref, sem.at[1]),
    ]
    queries = pltpu.make_async_copy(q_hbm, q_ref, sem.at[2])
    copies = []
    for w in range(2):
        for k in range(kv_used):
            cols = pl.ds(pl.multiple_of((kv_first() + k) * HEAD_DIM, HEAD_DIM), HEAD_DIM)
            part = w * kv_used + k
            rows = pl.ds(kv_at + part * tok_rows, tok_rows)
            copies.append(
                pltpu.make_async_copy(kv_hbm.at[w, :, cols], out_refs[1].at[rows, :], kv_sem.at[part])
            )
    for copy in tables + [queries] + copies:
        copy.start()
    for copy in tables:
        copy.wait()
    stored = owner_slots(pairs_ref, slots_ref)
    here = lax.axis_index("ctx")
    lanes = lax.broadcasted_iota(jnp.int32, (META_ROWS, HEAD_DIM), 1)
    blocks = []
    for distance, out_ref in enumerate(out_refs):
        owner = lax.rem(here + distance, ctx_count)
        block, counts = block_for(stored, owner, tiles_dev)
        blocks.append(block)
        meta = jnp.zeros((META_ROWS, HEAD_DIM), jnp.float32)
        for i, n in enumerate(counts):
            meta = jnp.where(lanes % tiles_dev == i, n.astype(jnp.float32), meta)
        out_ref[out_ref.shape[0] - META_ROWS :, :] = meta.astype(jnp.bfloat16)
    queries.wait()
    for block, out_ref in zip(blocks, out_refs):
        rows = pl.ds(pl.multiple_of(block * BLOCK, BLOCK), BLOCK)
        for h in range(heads):
            out_ref[h * BLOCK : (h + 1) * BLOCK, :] = q_ref[rows, h * HEAD_DIM : (h + 1) * HEAD_DIM]
    for copy in copies:
        copy.wait()


def pack_queries(pair_tiles, tile_slot, q_cross, kv_self, ctx_count, tiles_dev, kv_used, kv_first):
    rows = q_cross.shape[1] // HEAD_DIM * BLOCK + META_ROWS
    kv_rows = 2 * kv_used * kv_self.shape[1]
    return pl.pallas_call(
        functools.partial(pack_body, tiles_dev=tiles_dev, kv_used=kv_used, kv_first=kv_first),
        out_shape=[
            pltpu.VMEM((rows + (kv_rows if d == 1 else 0), HEAD_DIM), jnp.bfloat16)
            for d in range(ctx_count)
        ],
        in_specs=[HBM] * 4,
        out_specs=[VMEM] * ctx_count,
        scratch_shapes=[
            pltpu.VMEM(q_cross.shape, q_cross.dtype),
            pltpu.SMEM(pair_tiles.shape, jnp.int32),
            pltpu.SMEM(tile_slot.shape, jnp.int32),
            pltpu.SemaphoreType.DMA((2 * kv_used,)),
            pltpu.SemaphoreType.DMA((3,)),
        ],
        compiler_params=PARAMS,
        name="pack_queries",
    )(in_hbm(pair_tiles), in_hbm(tile_slot), in_hbm(q_cross), in_hbm(kv_self))


def count_bias(meta):
    count = meta[0:1, :].astype(jnp.float32)
    return jnp.where(count > 0, jnp.log(jnp.maximum(count, 1.0)) * LOG2E, NEG_FILL)


def finish_head(blended, total, best):
    live = total > 0
    total = jnp.where(live, total, 1.0)
    out = (blended / total).astype(jnp.bfloat16)
    lse = jnp.where(live, best * (1.0 / LOG2E) + jnp.log(total), NEG_FILL)
    return out, jnp.broadcast_to(lse, (lse.shape[0], HEAD_DIM))


def attend_head(q, meta, keys, values, key_count, wait_values):
    rows = q.shape[0]
    padded = keys.shape[0]
    lanes = HEAD_DIM
    bias = count_bias(meta)

    def score(at, size):
        return lax.dot_general(
            q, keys[at : at + size, :], (((1,), (1,)), ((), ())), preferred_element_type=jnp.float32
        )

    first = score(0, KEY_CHUNK)
    best = first[:, :lanes]
    for col in range(lanes, KEY_CHUNK, lanes):
        best = jnp.maximum(best, first[:, col : col + lanes])
    best = jnp.max(best * EXP2_SCALE + bias, axis=1, keepdims=True)
    shift = jnp.where(best > 0.5 * NEG_FILL, bias - best, NEG_FILL)
    totals = jnp.zeros((rows, lanes), jnp.float32)
    total = jnp.zeros((rows, 1), jnp.float32)
    blended = jnp.zeros((rows, HEAD_DIM), jnp.float32)
    waiting = []
    wait_values()
    for at in list(range(0, padded, KEY_CHUNK)) + [None] * LAG:
        if at is not None:
            size = min(KEY_CHUNK, padded - at)
            scores = score(at, size)
            pieces = []
            for col in range(0, size, lanes):
                width = min(lanes, size - col)
                weights = jnp.exp2(scores[:, col : col + width] * EXP2_SCALE + shift[:, :width])
                valid = key_count - at - col
                if width > valid:
                    held = lax.broadcasted_iota(jnp.int32, weights.shape, 1) < valid
                    weights = jnp.where(held, weights, 0.0)
                if width == lanes:
                    totals = totals + weights
                else:
                    total = total + jnp.sum(weights, axis=1, keepdims=True)
                pieces.append(weights.astype(jnp.bfloat16))
            weights = jnp.concatenate(pieces, axis=1) if len(pieces) > 1 else pieces[0]
            waiting.append((weights, at))
        if len(waiting) > LAG or at is None:
            weights, start = waiting.pop(0)
            blended = blended + jnp.dot(
                weights,
                values[start : start + weights.shape[1], :],
                preferred_element_type=jnp.float32,
            )
    total = total + jnp.sum(totals, axis=1, keepdims=True)
    return *finish_head(blended, total, best), total


def attend_head_exact(q, meta, keys, values, key_count, scores_sc):
    rows = q.shape[0]
    padded = keys.shape[0]
    lanes = HEAD_DIM
    bias = count_bias(meta)
    best = None
    for at in range(0, padded, KEY_CHUNK):
        size = min(KEY_CHUNK, padded - at)
        scores = lax.dot_general(
            q, keys[at : at + size, :], (((1,), (1,)), ((), ())), preferred_element_type=jnp.float32
        )
        for col in range(0, size, lanes):
            width = min(lanes, size - col)
            piece = scores[:, col : col + width]
            valid = key_count - at - col
            if width > valid:
                piece = jnp.where(lax.broadcasted_iota(jnp.int32, piece.shape, 1) < valid, piece, NEG_FILL)
            scores_sc[:, at + col : at + col + width] = piece
            if width == lanes:
                best = piece if best is None else jnp.maximum(best, piece)
            else:
                tail = piece
    best = jnp.max(best * EXP2_SCALE + bias, axis=1, keepdims=True)
    tail_width = padded % lanes
    if tail_width:
        tail = jnp.max(tail * EXP2_SCALE + bias[:, :tail_width], axis=1, keepdims=True)
        best = jnp.maximum(best, tail)
    shift = jnp.where(best > 0.5 * NEG_FILL, bias - best, NEG_FILL)
    totals = jnp.zeros((rows, lanes), jnp.float32)
    total = jnp.zeros((rows, 1), jnp.float32)
    blended = jnp.zeros((rows, HEAD_DIM), jnp.float32)
    for at in range(0, padded, KEY_CHUNK):
        size = min(KEY_CHUNK, padded - at)
        pieces = []
        for col in range(0, size, lanes):
            width = min(lanes, size - col)
            piece = scores_sc[:, at + col : at + col + width]
            weights = jnp.exp2(piece * EXP2_SCALE + shift[:, :width])
            if width == lanes:
                totals = totals + weights
            else:
                total = total + jnp.sum(weights, axis=1, keepdims=True)
            pieces.append(weights.astype(jnp.bfloat16))
        weights = jnp.concatenate(pieces, axis=1) if len(pieces) > 1 else pieces[0]
        blended = blended + jnp.dot(
            weights, values[at : at + size, :], preferred_element_type=jnp.float32
        )
    total = total + jnp.sum(totals, axis=1, keepdims=True)
    return finish_head(blended, total, best)


def attend_block(q_ref, keys_ref, values_ref, out_ref, lse_ref, scores_sc, key_count, wait):
    kv_used = keys_ref.shape[0]
    rows = scores_sc.shape[0]
    meta = q_ref[q_ref.shape[0] - META_ROWS :, :]

    def place(k):
        return slice(k * rows, (k + 1) * rows)

    def store(k, out, lse):
        out_ref[place(k), :] = out
        if lse_ref is not None:
            lse_ref[place(k), :] = lse

    highest = jnp.zeros((rows, 1), jnp.float32)
    for k in range(kv_used):
        wait_values = wait(k)
        keys, values = keys_ref.at[k], values_ref.at[k]
        out, lse, total = attend_head(q_ref[place(k), :], meta, keys, values, key_count, wait_values)
        store(k, out, lse)
        highest = jnp.maximum(highest, total)

    @pl.when(jnp.logical_not(jnp.max(highest) <= MOST_TOTAL))
    def _():
        for k in range(kv_used):
            keys, values = keys_ref.at[k], values_ref.at[k]
            store(
                k,
                *attend_head_exact(q_ref[place(k), :], meta, keys, values, key_count, scores_sc),
            )


def no_wait(k):
    return lambda: None


def own_body(q_ref, image_hbm, *refs, with_lse, kv_first):
    out_ref = refs[0]
    lse_ref = refs[1] if with_lse else None
    keys_ref, values_ref, scores_sc, sem = refs[-4:]
    _, tile_len, tiles_dev, width = image_hbm.shape
    key_count = tile_len * tiles_dev
    kv_used, padded = keys_ref.shape[:2]
    image = image_hbm.reshape(2, key_count, width)

    def copies(k):
        cols = pl.ds(pl.multiple_of((kv_first() + k) * HEAD_DIM, HEAD_DIM), HEAD_DIM)
        held = pl.ds(0, key_count)
        return [
            pltpu.make_async_copy(image.at[w, :, cols], ref.at[k, held], sem.at[w, k])
            for w, ref in enumerate((keys_ref, values_ref))
        ]

    if padded > key_count:
        pad = jnp.zeros((padded - key_count, HEAD_DIM), jnp.bfloat16)
        for k in range(kv_used):
            keys_ref[k, key_count:, :] = pad
            values_ref[k, key_count:, :] = pad
    for copy in copies(0):
        copy.start()

    def wait(k):
        keys, values = copies(k)
        keys.wait()
        if k == 0:
            for later in range(1, kv_used):
                for copy in copies(later):
                    copy.start()
        return values.wait

    attend_block(
        q_ref, keys_ref, values_ref, out_ref, lse_ref, scores_sc, key_count, wait
    )


def attend_own(packed, image_kv, kv_used, q_rows, with_lse, kv_first):
    _, tile_len, tiles_dev, _ = image_kv.shape
    padded = -(-tile_len * tiles_dev // 16) * 16
    held = pltpu.VMEM((kv_used, padded, HEAD_DIM), jnp.bfloat16)
    out_shape = [pltpu.VMEM((q_rows, HEAD_DIM), jnp.bfloat16)]
    if with_lse:
        out_shape.append(pltpu.VMEM((q_rows, HEAD_DIM), jnp.float32))
    out_shape += [held, held]
    results = pl.pallas_call(
        functools.partial(own_body, with_lse=with_lse, kv_first=kv_first),
        out_shape=out_shape,
        in_specs=[VMEM, HBM],
        out_specs=[VMEM] * len(out_shape),
        scratch_shapes=[
            pltpu.VMEM((q_rows // kv_used, padded), jnp.float32),
            pltpu.SemaphoreType.DMA((2, kv_used)),
        ],
        compiler_params=PARAMS,
        name="attend_own",
    )(in_vmem(packed), in_hbm(image_kv))
    return results[:-2], [in_vmem(part) for part in results[-2:]]


def arrived_body(q_ref, keys_ref, values_ref, out_ref, *refs, with_lse, key_count):
    lse_ref = refs[0] if with_lse else None
    attend_block(
        q_ref, keys_ref, values_ref, out_ref, lse_ref, refs[-1], key_count, no_wait
    )


def attend_arrived(packed, held, key_count, q_rows, with_lse):
    kv_used, padded, _ = held[0].shape
    out_shape = [pltpu.VMEM((q_rows, HEAD_DIM), jnp.bfloat16)]
    if with_lse:
        out_shape.append(pltpu.VMEM((q_rows, HEAD_DIM), jnp.float32))
    return pl.pallas_call(
        functools.partial(arrived_body, with_lse=with_lse, key_count=key_count),
        out_shape=out_shape,
        in_specs=[VMEM] * 3,
        out_specs=[VMEM] * len(out_shape),
        scratch_shapes=[pltpu.VMEM((q_rows // kv_used, padded), jnp.float32)],
        compiler_params=PARAMS,
        name="attend_arrived",
    )(in_vmem(packed), *held)


def join_body(partial_ref, message_ref, out_ref):
    q_rows = partial_ref.shape[0]
    out_ref[:q_rows, :] = partial_ref[...]
    out_ref[q_rows:, :] = message_ref[q_rows : out_ref.shape[0], :]


def join_keys(partial, message):
    return pl.pallas_call(
        join_body,
        out_shape=pltpu.VMEM((message.shape[0] - META_ROWS, HEAD_DIM), jnp.bfloat16),
        in_specs=[VMEM] * 2,
        out_specs=VMEM,
        compiler_params=PARAMS,
        name="join_keys",
    )(in_vmem(partial), in_vmem(message))


def self_body(docs_ref, q_ref, *refs, starts, kv_used):
    kv_refs, out_ref, bias_sc = refs[:-2], refs[-2], refs[-1]
    tok_rows, q_width = q_ref.shape
    per_kv = q_width // HEAD_DIM // kv_used
    shape = bias_sc.shape
    row_start = lax.axis_index("ctx") * tok_rows
    query_pos = row_start + lax.broadcasted_iota(jnp.int32, (tok_rows, 1), 0)
    key_pos = row_start + tok_rows - shape[1] + lax.broadcasted_iota(jnp.int32, shape, 1)
    doc_start = jnp.zeros((tok_rows, 1), jnp.int32)
    doc_end = jnp.int32(0)
    for j in range(docs_ref.shape[0]):
        doc_end = doc_end + docs_ref[j]
        doc_start = jnp.where(query_pos >= doc_end, doc_end, doc_start)
    bias_sc[...] = jnp.where((key_pos <= query_pos) & (key_pos >= doc_start), 0.0, NEG_FILL)
    for k in range(kv_used):
        keys, values = [
            jnp.concatenate(
                [
                    ref[at + (w * kv_used + k) * tok_rows : at + (w * kv_used + k + 1) * tok_rows, :]
                    for ref, at in zip(kv_refs, starts)
                ],
                axis=0,
            )
            for w in range(2)
        ]
        heads = range(k * per_kv, (k + 1) * per_kv)
        q = jnp.concatenate([q_ref[:, h * HEAD_DIM : (h + 1) * HEAD_DIM] for h in heads], axis=0)
        scores = lax.dot_general(
            q, keys, (((1,), (1,)), ((), ())), preferred_element_type=jnp.float32
        )
        scores = scores * EXP2_SCALE + jnp.concatenate([bias_sc[...]] * per_kv, axis=0)
        row_best = jnp.max(scores, axis=1, keepdims=True)
        weights = jnp.exp2(scores - row_best)
        row_total = jnp.sum(weights, axis=1, keepdims=True)
        blended = jnp.dot(weights.astype(jnp.bfloat16), values, preferred_element_type=jnp.float32)
        blended = blended / row_total
        for i, h in enumerate(heads):
            out_ref[:, h * HEAD_DIM : (h + 1) * HEAD_DIM] = blended[i * tok_rows : (i + 1) * tok_rows]


def attend_self(doc_lengths, q_self, pieces, kv_used):
    tok_rows, q_width = q_self.shape
    return pl.pallas_call(
        functools.partial(self_body, starts=[at for _, at in pieces], kv_used=kv_used),
        out_shape=pltpu.VMEM((tok_rows, q_width), jnp.float32),
        in_specs=[SMEM] + [VMEM] * (1 + len(pieces)),
        out_specs=VMEM,
        scratch_shapes=[pltpu.VMEM((tok_rows, len(pieces) * tok_rows), jnp.float32)],
        compiler_params=PARAMS,
        name="attend_self",
    )(doc_lengths, in_vmem(q_self), *[in_vmem(array) for array, _ in pieces])


def mix_blocks(blocks_ref, gate_ref, self_ref, partial_refs, distances, out_hbm, out_ref, sem):
    copies = []
    width = self_ref.shape[1]
    ends = [width // HEAD_DIM // 2, width // HEAD_DIM]
    for i, (distance, partial_ref) in enumerate(zip(distances, partial_refs)):
        rows = pl.ds(pl.multiple_of(blocks_ref[distance] * BLOCK, BLOCK), BLOCK)
        for h in range(self_ref.shape[1] // HEAD_DIM):
            cols = slice(h * HEAD_DIM, (h + 1) * HEAD_DIM)
            cross = partial_ref[h * BLOCK : (h + 1) * BLOCK, :].astype(jnp.float32)
            mixed = self_ref[rows, cols] + gate_ref[:, cols] * cross
            out_ref[i, :, cols] = mixed.astype(jnp.bfloat16)
            if h + 1 in ends:
                part = ends.index(h + 1)
                cols = pl.ds(part * width // 2, (h + 1) * HEAD_DIM - part * width // 2)
                copy = pltpu.make_async_copy(
                    out_ref.at[i, :, cols], out_hbm.at[rows, cols], sem.at[2 * i + part]
                )
                copy.start()
                copies.append(copy)
    for copy in copies:
        copy.wait()


def early_body(pairs_ref, slots_ref, gate_ref, self_ref, *refs, distances, tiles_dev):
    partial_refs, (out_hbm, blocks_ref, out_ref, sem) = refs[:-4], refs[-4:]
    stored = owner_slots(pairs_ref, slots_ref)
    here = lax.axis_index("ctx")
    ctx_count = blocks_ref.shape[0]
    for distance in range(ctx_count):
        owner = lax.rem(here + distance, ctx_count)
        blocks_ref[distance] = block_for(stored, owner, tiles_dev)[0]
    mix_blocks(blocks_ref, gate_ref, self_ref, partial_refs, distances, out_hbm, out_ref, sem)


def late_body(blocks_ref, gate_ref, self_ref, *refs, distances):
    partial_refs, (_, out_hbm, out_ref, sem) = refs[:-4], refs[-4:]
    mix_blocks(blocks_ref, gate_ref, self_ref, partial_refs, distances, out_hbm, out_ref, sem)


def mix(pair_tiles, tile_slot, gate_cols, self_out, partials, tiles_dev):
    ctx_count = len(partials)
    early, late = [0, ctx_count - 1], list(range(1, ctx_count - 1))
    out_shape = jax.ShapeDtypeStruct(self_out.shape, jnp.bfloat16)

    def scratch(distances):
        return [
            pltpu.VMEM((len(distances), BLOCK, self_out.shape[1]), jnp.bfloat16),
            pltpu.SemaphoreType.DMA((2 * len(distances),)),
        ]

    shared = (in_vmem(gate_cols), in_vmem(self_out))
    out, blocks = pl.pallas_call(
        functools.partial(early_body, distances=early, tiles_dev=tiles_dev),
        out_shape=[out_shape, pltpu.SMEM((ctx_count,), jnp.int32)],
        in_specs=[SMEM] * 2 + [VMEM] * (2 + len(early)),
        out_specs=[HBM, SMEM],
        scratch_shapes=scratch(early),
        compiler_params=PARAMS,
        name="mix_early",
    )(pair_tiles, tile_slot, *shared, *[in_vmem(partials[d]) for d in early])
    return pl.pallas_call(
        functools.partial(late_body, distances=late),
        out_shape=out_shape,
        in_specs=[SMEM] + [VMEM] * (2 + len(late)) + [HBM],
        out_specs=HBM,
        scratch_shapes=scratch(late),
        input_output_aliases={3 + len(late): 0},
        compiler_params=PARAMS,
        name="mix_late",
    )(
        pltpu.with_memory_space_constraint(blocks, pltpu.SMEM),
        *shared,
        *[in_vmem(partials[d]) for d in late],
        in_hbm(out),
    )


def mix_owners(pair_tiles, tile_slot, gate_cols, self_out, partials, sums, tiles_dev):
    block_count = pair_tiles.shape[0]
    tok_rows, q_width = self_out.shape
    heads = q_width // HEAD_DIM
    ctx_count = len(partials)
    owners = jnp.take(tile_slot, pair_tiles.reshape(-1), axis=0).reshape(block_count, -1) // tiles_dev
    partners = (lax.axis_index("ctx") + jnp.arange(ctx_count, dtype=jnp.int32)) % ctx_count
    live = jnp.any(owners[:, :, None] == partners[None, None, :], axis=1)[:, :, None, None]
    lse = jnp.stack(sums)[None]
    top = jnp.max(jnp.where(live, lse, NEG_FILL), axis=1, keepdims=True)
    factors = jnp.where(live, jnp.exp(lse - top), 0.0)
    pieces = jnp.stack(partials).astype(jnp.float32)[None]
    cross = jnp.sum(factors * pieces, axis=1) / jnp.sum(factors, axis=1)
    cross = jnp.transpose(cross.reshape(block_count, heads, BLOCK, HEAD_DIM), (0, 2, 1, 3))
    return (self_out + gate_cols * cross.reshape(tok_rows, q_width)).astype(jnp.bfloat16)


def partner_order(ctx_count):
    return list(range(ctx_count - 1, 0, -1))


def attend(q_self, q_cross, kv_self, image_kv, cross_gate, doc_lengths, pair_tiles, tile_slot):
    tok_rows, q_width = q_self.shape
    local_heads = q_width // HEAD_DIM
    q_rows = local_heads * BLOCK
    grouping = Q_HEADS // KV_HEADS
    per_kv = min(local_heads, grouping)
    kv_used = local_heads // per_kv
    ctx_count = lax.axis_size("ctx")
    tiles_dev, tile_len = image_kv.shape[1:3]
    request_count = pair_tiles.shape[0] * PAIRS
    capacity = max(2, -(-request_count // ctx_count))
    one_owner = ctx_count * capacity == request_count and capacity == PAIRS
    with_lse = not one_owner
    reach = min(ctx_count - 1, -(-(ctx_count * tok_rows // 2 - 1) // tok_rows))


    def kv_first():
        return lax.axis_index("rep") * local_heads // grouping

    image_kv = jnp.transpose(image_kv, (0, 2, 1, 3))

    def send(array, distance):
        pairs = [(i, (i + distance) % ctx_count) for i in range(ctx_count)]
        return lax.ppermute(array, "ctx", pairs)

    packed = pack_queries(
        pair_tiles, tile_slot, q_cross, kv_self, ctx_count, tiles_dev, kv_used, kv_first
    )
    last = ctx_count - 1
    order = partner_order(ctx_count)
    arrived = {d: send(packed[d], d) for d in order[-1:] + order[:-1]}
    results = {}
    results[0], held = attend_own(packed[0], image_kv, kv_used, q_rows, with_lse, kv_first)
    for d in order:
        answer = attend_arrived(arrived[d], held, tile_len * tiles_dev, q_rows, with_lse)
        if d == last:
            answer = [join_keys(answer[0], arrived[1]), *answer[1:]]
        results[d] = [send(part, ctx_count - d) for part in answer]

    pieces = [packed[1], arrived[1], results[last][0]][: reach + 1]
    pieces = [(piece, q_rows) for piece in pieces]
    for _ in range(len(pieces), reach + 1):
        array, first = pieces[-1]
        rows = 2 * kv_used * tok_rows
        pieces.append((send(array[first : first + rows], 1), 0))
    self_out = attend_self(doc_lengths, q_self, pieces[::-1], kv_used)
    gate_cols = jnp.repeat(jnp.tanh(cross_gate), HEAD_DIM)[None, :]
    partials = [results[d][0] for d in range(ctx_count)]
    if one_owner:
        return mix(pair_tiles, tile_slot, gate_cols, self_out, partials, tiles_dev)
    partials = [partial[:q_rows] for partial in partials]
    sums = [results[d][1] for d in range(ctx_count)]
    return mix_owners(pair_tiles, tile_slot, gate_cols, self_out, partials, sums, tiles_dev)


def solution(mesh):
    in_specs = (
        P(("groups", "ctx"), ("head", "rep")),
        P(("groups", "ctx"), ("head", "rep")),
        P(None, ("groups", "ctx"), "head"),
        P(None, ("groups", "ctx"), None, "head"),
        P(("head", "rep")),
        P("groups"),
        P(("groups", "ctx"), None),
        P("groups"),
    )
    out_specs = P(("groups", "ctx"), ("head", "rep"))
    return jax.shard_map(attend, mesh=mesh, in_specs=in_specs, out_specs=out_specs, check_vma=False)
```
